512 devices in a mesh: tm: 256 (over x_lo, z, y, core), space: 2 (over x_hi).
Axes of the slice: x: 4 (x_hi: 2, x_lo: 2; x = x_hi * 2 + x_lo), y: 8, z: 8, core: 2. Of those that a mesh axis runs over, the one named last changes fastest.
Arguments:
- control: float32 [32, 512], P('space'), may hold values from -0.6 to 0.6
- initial: float32 [32, 512], P('space'), may hold values from -6 to 6
- diffusion: float32 [32, 512], P('space'), may hold values from 0.1 to 1
- reaction: float32 [32, 512], P('space'), may hold values from 4.8828124e-06 to 0.1
- forward_guess: float32 [256, 32, 512], P('tm', 'space'), may hold values from -1.5 to 1.5
- adjoint_guess: float32 [256, 32, 512], P('tm', 'space'), may hold values from -1.5 to 1.5
- observed: float32 [256, 32, 512], P('tm', 'space'), may hold values from -6 to 6
Outputs:
- forward_states: float32 [256, 32, 512], P('tm', 'space')
- adjoint_states: float32 [256, 32, 512], P('tm', 'space')
- control_gradient: float32 [32, 512], P('space')
The draws below stay inside these ranges and needn't reach their ends.
All inputs are finite; a program needn't handle non-finite values.
Results may differ from the reference program's by a relative error of at most 0.00015.
Values sent between devices are 32-bit elements; how exact they have to be, the bound alone decides.
No kernel may reach another device: no remote copies, remote signals or barrier semaphores. Data moves between devices by JAX's collectives and lax.ppermute only.
A program may use at most 128 MiB of HBM per device.

```python
import math
import jax
import jax.numpy as jnp
from jax import lax

COLS = 512
SWEEPS = 3
COARSEN = 8
SLABS = 256
NX = 32
STEPS = 2048


def shard_levels(key, extent, pieces, low, top_value):
    loudness, own = 1.0, jax.random.fold_in(key, 6)
    for axis_at, parts in pieces:
        heights = jnp.exp(jax.random.uniform(jax.random.fold_in(own, axis_at), (parts,), jnp.float32, low / len(pieces), top_value / len(pieces)))
        loudness = loudness * jnp.repeat(heights, extent[axis_at] // parts).reshape([-1 if axis == axis_at else 1 for axis in range(len(extent))])
    return loudness


def gaussian(stream_key, extent, width, bound, pieces=(), dtype=jnp.bfloat16):
    level = shard_levels(stream_key, extent, pieces, -0.22, 0.18) if pieces else 1.0
    array = jax.random.normal(stream_key, extent, jnp.float32) * width * level
    return jnp.minimum(jnp.maximum(array, -bound), bound).astype(dtype)


def setup_inputs(seed: int = 0) -> dict:
    streams_of = jax.random.split(jax.random.key(seed), 8)
    control = gaussian(streams_of[0], (NX, COLS), 0.1, 0.6, ((0, 2),), jnp.float32)
    initial = gaussian(streams_of[1], (NX, COLS), 1.0, 6.0, ((0, 2),), jnp.float32)
    diffusion = jnp.clip(jnp.exp(math.log(1.0) - 2.3025851 * jax.random.uniform(streams_of[2], (NX, COLS), jnp.float32) ** shard_levels(streams_of[2], (NX, COLS), ((0, 2),), -0.2, 0.2)), 0.1, 1.0)
    reaction = jnp.clip(jnp.exp(math.log(0.1) - 9.927204 * jax.random.uniform(streams_of[3], (NX, COLS), jnp.float32) ** shard_levels(streams_of[3], (NX, COLS), ((0, 2),), -0.2, 0.2)), 4.882812390860636e-06, 0.1)
    forward_guess = gaussian(streams_of[4], (SLABS, NX, COLS), 0.25, 1.5, ((0, 256), (1, 2)), jnp.float32)
    adjoint_guess = gaussian(streams_of[5], (SLABS, NX, COLS), 0.25, 1.5, ((0, 256), (1, 2)), jnp.float32)
    observed = gaussian(streams_of[6], (SLABS, NX, COLS), 1.0, 6.0, ((0, 256), (1, 2)), jnp.float32)
    return dict(control=control, initial=initial, diffusion=diffusion, reaction=reaction, forward_guess=forward_guess, adjoint_guess=adjoint_guess, observed=observed)


def neighbours(source):
    zero_row = jnp.zeros_like(source[..., :1, :])
    zero_column = jnp.zeros_like(source[..., :, :1])
    vertical = jnp.concatenate([source[..., 1:, :], zero_row], -2) + jnp.concatenate([zero_row, source[..., :-1, :]], -2)
    lateral = jnp.concatenate([source[..., :, 1:], zero_column], -1) + jnp.concatenate([zero_column, source[..., :, :-1]], -1)
    return vertical + lateral


def reference(control, initial, diffusion, reaction, forward_guess, adjoint_guess, observed):
    diagonal = 1.0 + 4.0 * diffusion + reaction
    weight = diffusion / diagonal

    def forward_map(rhs_field):
        iterate = rhs_field
        for number in range(SWEEPS):
            iterate = (rhs_field + diffusion * neighbours(iterate)) / diagonal
        return iterate

    def adjoint_map(rhs_field):
        carried = rhs_field
        summed = rhs_field
        for number in range(SWEEPS - 1):
            carried = neighbours(weight * carried)
            summed = summed + carried
        return summed / diagonal + neighbours(weight * carried)

    zero_slab = jnp.zeros_like(forward_guess[:1])

    def relax(own_forward, own_adjoint, first_pass):
        current = jnp.concatenate([initial[None], own_forward[:-1]], 0)
        states = []
        for number in range(COARSEN - 1):
            current = forward_map(current + control)
            states.append(current)
        points = states + [own_forward]
        current = jnp.concatenate([own_adjoint[1:], zero_slab], 0)
        fine_total = jnp.zeros_like(own_adjoint)
        for position in range(COARSEN, 1, -1):
            current = adjoint_map(current + (points[position - 1] - observed) / COARSEN)
            fine_total = fine_total + current
        if first_pass:
            forward_residual = forward_map(states[-1] + control) - own_forward
            adjoint_residual = adjoint_map(current + (points[0] - observed) / COARSEN) - own_adjoint
            return forward_residual, adjoint_residual
        return fine_total

    forward_residual, adjoint_residual = relax(forward_guess, adjoint_guess, True)
    damping = 1.0 / (1.0 + COARSEN * reaction)

    def coarse_chain(running, increment):
        running = damping * running + increment
        return running, running

    zero_field = jnp.zeros_like(initial)
    forward_correction = lax.scan(coarse_chain, zero_field, forward_residual)[1]
    adjoint_correction = lax.scan(coarse_chain, zero_field, adjoint_residual, reverse=True)[1]
    forward_states = forward_guess + forward_correction
    adjoint_states = adjoint_guess + adjoint_correction
    fine_total = relax(forward_states, adjoint_states, False)
    control_gradient = (jnp.sum(adjoint_states, 0) + jnp.sum(fine_total, 0)) / STEPS
    return forward_states, adjoint_states, control_gradient
```

```python
import jax
import jax.numpy as jnp
from jax import lax
from jax.experimental import pallas as pl
from jax.experimental.pallas import tpu as pltpu
from jax.sharding import Mesh
from jax.sharding import PartitionSpec as P

SWEEPS = 3
COARSEN = 8
SLABS = 256
TM = ("tm_0", "tm_1", "tm_2", "tm_3")
ROWS = 16
COLS = 512
LANES = 128
TILES = COLS // LANES
PHASES = 4

ENTRY, FORWARD, ADJOINT, TARGET, CONTROL, SPREAD, REACTION = range(7)
WEIGHT, INVERSE, DAMPING, ALPHA, BETA, GAMMA, SOURCE, STATE, TOTAL, FW_LESS, AD_LESS = range(11)


def tm_index():
    return ((lax.axis_index("tm_0") * 8 + lax.axis_index("tm_1")) * 8 + lax.axis_index("tm_2")) * 2 + lax.axis_index(
        "tm_3"
    )


def each(fn, *fields):
    return [[fn(*(f[p][t] for f in fields)) for t in range(TILES)] for p in range(PHASES)]


def load(ref, *at):
    return [[ref[(*at, p, slice(None), pl.ds(t * LANES, LANES))] for t in range(TILES)] for p in range(PHASES)]


def store(value, ref, *at):
    for p in range(PHASES):
        for t in range(TILES):
            ref[(*at, p, slice(None), pl.ds(t * LANES, LANES))] = value[p][t]


def make_neighbours(space):
    sub = lax.broadcasted_iota(jnp.int32, (8, LANES), 0)
    lane = lax.broadcasted_iota(jnp.int32, (8, LANES), 1)
    up_ok = sub != 4 * space
    down_ok = sub != 7 - 4 * space
    first, last = (lane == 0, lane == LANES - 1)

    def neighbours(v):
        above = [jnp.where(up_ok, pltpu.roll(v[PHASES - 1][t], 1, 0), 0.0) for t in range(TILES)]
        below = [jnp.where(down_ok, pltpu.roll(v[0][t], 7, 0), 0.0) for t in range(TILES)]
        out = []
        for p in range(PHASES):
            ups = v[p - 1] if p else above
            downs = v[p + 1] if p < PHASES - 1 else below
            right = [pltpu.roll(v[p][t], 1, 1) for t in range(TILES)]
            left = [pltpu.roll(v[p][t], LANES - 1, 1) for t in range(TILES)]
            row = []
            for t in range(TILES):
                a = jnp.where(first, right[t - 1] if t else 0.0, right[t])
                b = jnp.where(last, left[t + 1] if t < TILES - 1 else 0.0, left[t])
                row.append((ups[t] + downs[t]) + (a + b))
            out.append(row)
        return out

    return neighbours


def relax_kernel(own_ref, other_ref, chan_ref, keep_ref, raw, grid, field, points, coarse_points):
    slab = tm_index()
    space = lax.axis_index("space")
    neighbours = make_neighbours(space)
    is_last = slab == SLABS - 1
    not_last = jnp.where(is_last, 0.0, 1.0)
    not_first = jnp.where(slab == 0, 0.0, 1.0)

    for n in range(7):
        for t in range(TILES):
            cols = pl.ds(t * LANES, LANES)
            raw[n, t, 0:ROWS, :] = own_ref[n, :, cols]
            raw[n, t, ROWS : 2 * ROWS, :] = other_ref[n, :, cols]
    for n in range(7):
        for p in range(PHASES):
            for t in range(TILES):
                grid[n, p, :, pl.ds(t * LANES, LANES)] = raw[n, t, pl.ds(p, 8, stride=PHASES), :]

    spread, reaction = (load(grid, SPREAD), load(grid, REACTION))
    inverse = each(lambda s, r: 1.0 / (1.0 + 4.0 * s + r), spread, reaction)
    store(inverse, field, INVERSE)
    store(each(lambda s, i: s * i, spread, inverse), field, WEIGHT)
    store(each(lambda r: 1.0 / (1.0 + COARSEN * r), reaction), field, DAMPING)

    def forward_step(right_side):
        weight, scaled = (load(field, WEIGHT), each(lambda r, i: r * i, right_side, load(field, INVERSE)))
        v = right_side
        for _ in range(SWEEPS):
            v = each(lambda s, w, n: s + w * n, scaled, weight, neighbours(v))
        return v

    def adjoint_step(y):
        weight = load(field, WEIGHT)
        carried, summed = (y, y)
        for _ in range(SWEEPS - 1):
            carried = neighbours(each(jnp.multiply, weight, carried))
            summed = each(jnp.add, summed, carried)
        final = neighbours(each(jnp.multiply, weight, carried))
        return each(lambda s, i, f: s * i + f, summed, load(field, INVERSE), final)

    store(load(grid, ENTRY), field, STATE)

    def forward_body(i, _):
        v = forward_step(each(jnp.add, load(field, STATE), load(grid, CONTROL)))
        store(v, field, STATE)
        store(v, points, i)
        return 0

    lax.fori_loop(0, COARSEN, forward_body, 0)

    damping = load(field, DAMPING)
    forward_less = jnp.where(is_last, SLABS - 1, SLABS - 2 - slab)
    adjoint_less = jnp.maximum(slab - 1, 0)
    for slot, count in ((FW_LESS, forward_less), (AD_LESS, adjoint_less)):
        power, block = (damping, each(jnp.ones_like, damping))
        total = each(jnp.zeros_like, damping)
        for b in range(8):
            taken = ((count >> b) & 1) == 1
            total = each(lambda s, v, q: jnp.where(taken, v + q * s, s), total, block, power)
            if b < 7:
                block = each(lambda v, q: v + v * q, block, power)
                power = each(lambda q: q * q, power)
        store(total, field, slot)

    push = each(
        lambda f, d, g: f - not_last * (d * g), load(field, STATE), damping, load(grid, FORWARD)
    )
    store(push, field, SOURCE)
    store(
        each(lambda w, u, e: w * u + (1.0 - not_last) * e, load(field, FW_LESS), push, load(grid, ENTRY)),
        field,
        STATE,
    )
    store(each(jnp.zeros_like, damping), field, ALPHA)
    store(load(grid, ADJOINT), field, BETA)
    store(each(lambda g: g / COARSEN, load(grid, FORWARD)), field, GAMMA)

    def adjoint_body(n, _):
        at = COARSEN - 1 - n
        share = jnp.where(n == 0, 0.0, 1.0 / COARSEN)
        store(adjoint_step(each(lambda a, f: a + share * f, load(field, ALPHA), load(points, at))), field, ALPHA)
        store(adjoint_step(load(field, BETA)), field, BETA)
        store(
            adjoint_step(each(lambda a, o: a - o / COARSEN, load(field, GAMMA), load(grid, TARGET))), field, GAMMA
        )
        v = forward_step(each(jnp.add, load(field, STATE), load(grid, CONTROL)))
        store(v, field, STATE)
        store(v, coarse_points, n)
        return 0

    lax.fori_loop(0, COARSEN, adjoint_body, 0)

    damping = load(field, DAMPING)
    alpha, beta, gamma = (load(field, ALPHA), load(field, BETA), load(field, GAMMA))
    keep = each(lambda g, d, a: g + not_last * (d * a), gamma, damping, alpha)
    pull = each(
        lambda k, d, g, b: d * (k - g) + b, keep, damping, load(grid, ADJOINT), beta
    )
    push = load(field, SOURCE)
    less = load(field, AD_LESS)
    store(
        each(lambda a, k, w, q, d: a + k + not_first * ((1.0 + d * w) * q), alpha, keep, less, pull, damping),
        field,
        TOTAL,
    )
    rest = each(lambda a, k, w, q: not_last * a + not_first * (k + w * q), alpha, keep, less, pull)
    store(
        each(
            lambda t, w, d, u, o: t + ((1.0 + d * w) * u - o) / COARSEN,
            rest,
            load(field, FW_LESS),
            damping,
            push,
            load(grid, TARGET),
        ),
        field,
        GAMMA,
    )
    store(pull, field, BETA)
    store(keep, field, STATE)

    def gradient_body(n, _):
        v = adjoint_step(load(field, GAMMA))
        store(each(jnp.add, load(field, TOTAL), v), field, TOTAL)
        at = COARSEN - 2 - n
        store(
            each(lambda a, f, o: a + (f - o) / COARSEN, v, load(coarse_points, at), load(grid, TARGET)), field, GAMMA
        )
        return 0

    lax.fori_loop(0, COARSEN - 1, gradient_body, 0)

    for n, slot in enumerate((SOURCE, BETA, ALPHA, TOTAL)):
        for p in range(PHASES):
            for t in range(TILES):
                block = field[slot, p, 0:4, pl.ds(t * LANES, LANES)]
                chan_ref[pl.ds((n * TILES + t) * ROWS + p, 4, stride=PHASES), :] = block
    for p in range(PHASES):
        for t in range(TILES):
            keep_ref[pl.ds(t * ROWS + p, 4, stride=PHASES), :] = field[STATE, p, 0:4, pl.ds(t * LANES, LANES)]


def chain_kernel(got_ref, reaction_ref, out_ref):
    owner = tm_index()
    role = owner // 64
    cell = owner % 64
    tile = cell // ROWS
    row = reaction_ref[pl.ds(cell % ROWS, 1), :]
    reaction = row[:, 0:LANES]
    for t in range(1, TILES):
        reaction = jnp.where(tile == t, row[:, t * LANES : (t + 1) * LANES], reaction)
    d = jnp.broadcast_to(1.0 / (1.0 + COARSEN * reaction), (8, LANES))
    length = SLABS // 8
    sub = lax.broadcasted_iota(jnp.int32, (8, LANES), 0)
    d32 = d
    for _ in range(5):
        d32 = d32 * d32
    d64 = d32 * d32
    d128 = d64 * d64

    def strided(i):
        return pl.ds(i, 8, stride=length)

    @pl.when(role == 0)
    def _():
        x = pltpu.roll(got_ref[strided(length - 1), :], 1, 0)
        local = [x]
        for i in range(1, length):
            x = d * x + got_ref[strided(i - 1), :]
            local.append(x)
        c = x
        c = c + jnp.where(sub >= 1, d32 * pltpu.roll(c, 1, 0), 0.0)
        c = c + jnp.where(sub >= 2, d64 * pltpu.roll(c, 2, 0), 0.0)
        c = c + jnp.where(sub >= 4, d128 * pltpu.roll(c, 4, 0), 0.0)
        c = jnp.where(sub >= 1, pltpu.roll(c, 1, 0), 0.0)
        for i in range(length):
            c = d * c
            out_ref[strided(i), :] = local[i] + c

    @pl.when(role == 1)
    def _():
        x = jnp.where(sub == 7, 0.0, pltpu.roll(got_ref[strided(0), :], 7, 0))
        local = [x]
        for i in range(length - 2, -1, -1):
            x = d * x + got_ref[strided(i + 1), :]
            local.append(x)
        c = x
        c = c + jnp.where(sub < 7, d32 * pltpu.roll(c, 7, 0), 0.0)
        c = c + jnp.where(sub < 6, d64 * pltpu.roll(c, 6, 0), 0.0)
        c = c + jnp.where(sub < 4, d128 * pltpu.roll(c, 4, 0), 0.0)
        c = jnp.where(sub < 7, pltpu.roll(c, 7, 0), 0.0)
        for n in range(length):
            c = d * c
            out_ref[strided(length - 1 - n), :] = local[n] + c

    @pl.when(role == 2)
    def _():
        out_ref[strided(0), :] = pltpu.roll(got_ref[strided(length - 1), :], 1, 0)
        for i in range(1, length):
            out_ref[strided(i), :] = got_ref[strided(i - 1), :]

    @pl.when(role == 3)
    def _():
        parts = [got_ref[pl.ds(8 * i, 8), :] for i in range(length)]
        while len(parts) > 1:
            parts = [a + b for a, b in zip(parts[::2], parts[1::2])]
        total = jnp.sum(parts[0], axis=0, keepdims=True) * (1.0 / (COARSEN * SLABS))
        total = jnp.broadcast_to(total, (8, LANES))
        for i in range(length):
            out_ref[pl.ds(8 * i, 8), :] = total


def finish_kernel(got_ref, keep_ref, forward_ref, adjoint_ref, gradient_ref):
    for t in range(TILES):
        cols = pl.ds(t * LANES, LANES)
        forward, scanned, passed, gradient = (got_ref[pl.ds(64 * n + t * ROWS, ROWS), :] for n in range(4))
        forward_ref[:, cols] = forward
        adjoint_ref[:, cols] = scanned + (passed + keep_ref[pl.ds(t * ROWS, ROWS), :])
        gradient_ref[:, cols] = gradient


def in_vmem(count):
    return [pl.BlockSpec(memory_space=pltpu.VMEM)] * count


def field_shape(*lead):
    return pltpu.VMEM((*lead, PHASES, 8, COLS), jnp.float32)


def shards(control, initial, diffusion, reaction, forward_guess, adjoint_guess, observed):
    own_forward = forward_guess[0]
    entry = jnp.where(tm_index() == SLABS - 1, initial, own_forward)
    own = jnp.stack((entry, own_forward, adjoint_guess[0], observed[0], control, diffusion, reaction))
    other = lax.ppermute(own, "space", [(0, 1), (1, 0)])
    block = jax.ShapeDtypeStruct((ROWS, COLS), jnp.float32)
    rows = jax.ShapeDtypeStruct((SLABS, LANES), jnp.float32)
    channels, keep = pl.pallas_call(
        relax_kernel,
        out_shape=(rows, jax.ShapeDtypeStruct((64, LANES), jnp.float32)),
        in_specs=in_vmem(2),
        out_specs=in_vmem(2),
        scratch_shapes=[
            pltpu.VMEM((7, TILES, 2 * ROWS, LANES), jnp.float32),
            field_shape(7),
            field_shape(11),
            field_shape(COARSEN),
            field_shape(COARSEN),
        ],
        name="relax",
    )(own, other)
    got = lax.all_to_all(channels, TM, 0, 0, tiled=True)
    sent = pl.pallas_call(
        chain_kernel, out_shape=rows, in_specs=in_vmem(2), out_specs=in_vmem(1)[0], name="chain"
    )(got, reaction)
    back = lax.all_to_all(sent, TM, 0, 0, tiled=True)
    forward_states, adjoint_states, gradient = pl.pallas_call(
        finish_kernel, out_shape=(block, block, block), in_specs=in_vmem(2), out_specs=in_vmem(3), name="finish"
    )(back, keep)
    return (forward_states[None], adjoint_states[None], gradient)


def solution(mesh):
    finer = Mesh(
        mesh.devices.reshape(2, 8, 8, 2, mesh.shape["space"]),
        ("tm_0", "tm_1", "tm_2", "tm_3", "space"),
    )
    return jax.shard_map(
        shards,
        mesh=finer,
        in_specs=(
            P("space", None),
            P("space", None),
            P("space", None),
            P("space", None),
            P(TM, "space", None),
            P(TM, "space", None),
            P(TM, "space", None),
        ),
        out_specs=(P(TM, "space", None), P(TM, "space", None), P("space", None)),
        check_vma=False,
    )
```

```python
import jax
import jax.numpy as jnp
from jax import lax
from jax.experimental import pallas as pl
from jax.experimental.pallas import tpu as pltpu
from jax.sharding import Mesh
from jax.sharding import PartitionSpec as P

SWEEPS = 3
COARSEN = 8
SLABS = 256
TM = ("tm_0", "tm_1", "tm_2", "tm_3")
ROWS = 16
COLS = 512
LANES = 128
TILES = COLS // LANES
PHASES = 4

ENTRY, FORWARD, ADJOINT, TARGET, CONTROL, SPREAD, REACTION = range(7)
WEIGHT, INVERSE, DAMPING, ALPHA, BETA, GAMMA, SOURCE, STATE, TOTAL, FW_LESS, AD_LESS = range(11)


def tm_index():
    return ((lax.axis_index("tm_0") * 8 + lax.axis_index("tm_1")) * 8 + lax.axis_index("tm_2")) * 2 + lax.axis_index(
        "tm_3"
    )


def space_index():
    return lax.axis_index("space")


def each(fn, *fields):
    return [[fn(*(f[p][t] for f in fields)) for t in range(TILES)] for p in range(PHASES)]


def load(ref, *at):
    return [[ref[(*at, p, slice(None), pl.ds(t * LANES, LANES))] for t in range(TILES)] for p in range(PHASES)]


def store(value, ref, *at):
    for p in range(PHASES):
        for t in range(TILES):
            ref[(*at, p, slice(None), pl.ds(t * LANES, LANES))] = value[p][t]


def make_neighbours(space):
    sub = lax.broadcasted_iota(jnp.int32, (8, LANES), 0)
    lane = lax.broadcasted_iota(jnp.int32, (8, LANES), 1)
    up_ok = sub != 4 * space
    down_ok = sub != 7 - 4 * space
    first, last = (lane == 0, lane == LANES - 1)

    def neighbours(v):
        above = [jnp.where(up_ok, pltpu.roll(v[PHASES - 1][t], 1, 0), 0.0) for t in range(TILES)]
        below = [jnp.where(down_ok, pltpu.roll(v[0][t], 7, 0), 0.0) for t in range(TILES)]
        out = []
        for p in range(PHASES):
            ups = v[p - 1] if p else above
            downs = v[p + 1] if p < PHASES - 1 else below
            right = [pltpu.roll(v[p][t], 1, 1) for t in range(TILES)]
            left = [pltpu.roll(v[p][t], LANES - 1, 1) for t in range(TILES)]
            row = []
            for t in range(TILES):
                a = jnp.where(first, right[t - 1] if t else 0.0, right[t])
                b = jnp.where(last, left[t + 1] if t < TILES - 1 else 0.0, left[t])
                row.append((ups[t] + downs[t]) + (a + b))
            out.append(row)
        return out

    return neighbours


def pack_kernel(control, initial, diffusion, reaction, forward, adjoint, observed, out_ref, sems):
    is_last = tm_index() == SLABS - 1

    def copy(source, slot):
        return pltpu.make_async_copy(source, out_ref.at[slot], sems.at[slot])

    @pl.when(is_last)
    def _():
        copy(initial, ENTRY).start()

    @pl.when(jnp.logical_not(is_last))
    def _():
        copy(forward, ENTRY).start()

    rest = (
        (forward, FORWARD),
        (adjoint, ADJOINT),
        (observed, TARGET),
        (control, CONTROL),
        (diffusion, SPREAD),
        (reaction, REACTION),
    )
    for source, slot in rest:
        copy(source, slot).start()
    copy(forward, ENTRY).wait()
    for source, slot in rest:
        copy(source, slot).wait()


def relax_kernel(own_ref, other_ref, chan_ref, keep_ref, raw, grid, field, points, coarse_points):
    slab = tm_index()
    space = space_index()
    neighbours = make_neighbours(space)
    is_last = slab == SLABS - 1
    not_last = jnp.where(is_last, 0.0, 1.0)
    not_first = jnp.where(slab == 0, 0.0, 1.0)

    for n in range(7):
        for t in range(TILES):
            cols = pl.ds(t * LANES, LANES)
            raw[n, t, 0:ROWS, :] = own_ref[n, :, cols]
            raw[n, t, ROWS : 2 * ROWS, :] = other_ref[n, :, cols]
    for n in range(7):
        for p in range(PHASES):
            for t in range(TILES):
                grid[n, p, :, pl.ds(t * LANES, LANES)] = raw[n, t, pl.ds(p, 8, stride=PHASES), :]

    spread, reaction = (load(grid, SPREAD), load(grid, REACTION))
    inverse = each(lambda s, r: 1.0 / (1.0 + 4.0 * s + r), spread, reaction)
    store(inverse, field, INVERSE)
    store(each(lambda s, i: s * i, spread, inverse), field, WEIGHT)
    store(each(lambda r: 1.0 / (1.0 + COARSEN * r), reaction), field, DAMPING)

    def forward_step(right_side):
        weight, scaled = (load(field, WEIGHT), each(lambda r, i: r * i, right_side, load(field, INVERSE)))
        v = right_side
        for _ in range(SWEEPS):
            v = each(lambda s, w, n: s + w * n, scaled, weight, neighbours(v))
        return v

    def adjoint_step(y):
        weight = load(field, WEIGHT)
        carried, summed = (y, y)
        for _ in range(SWEEPS - 1):
            carried = neighbours(each(jnp.multiply, weight, carried))
            summed = each(jnp.add, summed, carried)
        final = neighbours(each(jnp.multiply, weight, carried))
        return each(lambda s, i, f: s * i + f, summed, load(field, INVERSE), final)

    store(load(grid, ENTRY), field, STATE)

    def forward_body(i, _):
        v = forward_step(each(jnp.add, load(field, STATE), load(grid, CONTROL)))
        store(v, field, STATE)
        store(v, points, i)
        return 0

    lax.fori_loop(0, COARSEN, forward_body, 0)

    damping = load(field, DAMPING)
    forward_less = jnp.where(is_last, SLABS - 1, SLABS - 2 - slab)
    adjoint_less = jnp.maximum(slab - 1, 0)
    for slot, count in ((FW_LESS, forward_less), (AD_LESS, adjoint_less)):
        power, block = (damping, each(jnp.ones_like, damping))
        total = each(jnp.zeros_like, damping)
        for b in range(8):
            taken = ((count >> b) & 1) == 1
            total = each(lambda s, v, q: jnp.where(taken, v + q * s, s), total, block, power)
            if b < 7:
                block = each(lambda v, q: v + v * q, block, power)
                power = each(lambda q: q * q, power)
        store(total, field, slot)

    push = each(
        lambda f, d, g: f - not_last * (d * g), load(field, STATE), damping, load(grid, FORWARD)
    )
    store(push, field, SOURCE)
    store(
        each(lambda w, u, e: w * u + (1.0 - not_last) * e, load(field, FW_LESS), push, load(grid, ENTRY)),
        field,
        STATE,
    )
    store(each(jnp.zeros_like, damping), field, ALPHA)
    store(load(grid, ADJOINT), field, BETA)
    store(each(lambda g: g / COARSEN, load(grid, FORWARD)), field, GAMMA)

    def adjoint_body(n, _):
        at = COARSEN - 1 - n
        share = jnp.where(n == 0, 0.0, 1.0 / COARSEN)
        store(adjoint_step(each(lambda a, f: a + share * f, load(field, ALPHA), load(points, at))), field, ALPHA)
        store(adjoint_step(load(field, BETA)), field, BETA)
        store(
            adjoint_step(each(lambda a, o: a - o / COARSEN, load(field, GAMMA), load(grid, TARGET))), field, GAMMA
        )
        v = forward_step(each(jnp.add, load(field, STATE), load(grid, CONTROL)))
        store(v, field, STATE)
        store(v, coarse_points, n)
        return 0

    lax.fori_loop(0, COARSEN, adjoint_body, 0)

    damping = load(field, DAMPING)
    alpha, beta, gamma = (load(field, ALPHA), load(field, BETA), load(field, GAMMA))
    keep = each(lambda g, d, a: g + not_last * (d * a), gamma, damping, alpha)
    pull = each(
        lambda k, d, g, b: d * (k - g) + b, keep, damping, load(grid, ADJOINT), beta
    )
    push = load(field, SOURCE)
    less = load(field, AD_LESS)
    store(
        each(lambda a, k, w, q, d: a + k + not_first * ((1.0 + d * w) * q), alpha, keep, less, pull, damping),
        field,
        TOTAL,
    )
    rest = each(lambda a, k, w, q: not_last * a + not_first * (k + w * q), alpha, keep, less, pull)
    store(
        each(
            lambda t, w, d, u, o: t + ((1.0 + d * w) * u - o) / COARSEN,
            rest,
            load(field, FW_LESS),
            damping,
            push,
            load(grid, TARGET),
        ),
        field,
        GAMMA,
    )
    store(pull, field, BETA)
    store(keep, field, STATE)

    def gradient_body(n, _):
        v = adjoint_step(load(field, GAMMA))
        store(each(jnp.add, load(field, TOTAL), v), field, TOTAL)
        at = COARSEN - 2 - n
        store(
            each(lambda a, f, o: a + (f - o) / COARSEN, v, load(coarse_points, at), load(grid, TARGET)), field, GAMMA
        )
        return 0

    lax.fori_loop(0, COARSEN - 1, gradient_body, 0)

    for n, slot in enumerate((SOURCE, BETA, ALPHA, TOTAL)):
        for p in range(PHASES):
            for t in range(TILES):
                block = field[slot, p, 0:4, pl.ds(t * LANES, LANES)]
                chan_ref[pl.ds((n * TILES + t) * ROWS + p, 4, stride=PHASES), :] = block
    for p in range(PHASES):
        for t in range(TILES):
            keep_ref[pl.ds(t * ROWS + p, 4, stride=PHASES), :] = field[STATE, p, 0:4, pl.ds(t * LANES, LANES)]


def chain_kernel(got_ref, own_ref, out_ref):
    owner = tm_index()
    role = owner // 64
    cell = owner % 64
    tile = cell // ROWS
    row = own_ref[REACTION, pl.ds(cell % ROWS, 1), :]
    reaction = row[:, 0:LANES]
    for t in range(1, TILES):
        reaction = jnp.where(tile == t, row[:, t * LANES : (t + 1) * LANES], reaction)
    d = jnp.broadcast_to(1.0 / (1.0 + COARSEN * reaction), (8, LANES))
    length = SLABS // 8
    sub = lax.broadcasted_iota(jnp.int32, (8, LANES), 0)
    d32 = d
    for _ in range(5):
        d32 = d32 * d32
    d64 = d32 * d32
    d128 = d64 * d64

    def strided(i):
        return pl.ds(i, 8, stride=length)

    @pl.when(role == 0)
    def _():
        x = pltpu.roll(got_ref[strided(length - 1), :], 1, 0)
        local = [x]
        for i in range(1, length):
            x = d * x + got_ref[strided(i - 1), :]
            local.append(x)
        c = x
        c = c + jnp.where(sub >= 1, d32 * pltpu.roll(c, 1, 0), 0.0)
        c = c + jnp.where(sub >= 2, d64 * pltpu.roll(c, 2, 0), 0.0)
        c = c + jnp.where(sub >= 4, d128 * pltpu.roll(c, 4, 0), 0.0)
        c = jnp.where(sub >= 1, pltpu.roll(c, 1, 0), 0.0)
        for i in range(length):
            c = d * c
            out_ref[strided(i), :] = local[i] + c

    @pl.when(role == 1)
    def _():
        x = jnp.where(sub == 7, 0.0, pltpu.roll(got_ref[strided(0), :], 7, 0))
        local = [x]
        for i in range(length - 2, -1, -1):
            x = d * x + got_ref[strided(i + 1), :]
            local.append(x)
        c = x
        c = c + jnp.where(sub < 7, d32 * pltpu.roll(c, 7, 0), 0.0)
        c = c + jnp.where(sub < 6, d64 * pltpu.roll(c, 6, 0), 0.0)
        c = c + jnp.where(sub < 4, d128 * pltpu.roll(c, 4, 0), 0.0)
        c = jnp.where(sub < 7, pltpu.roll(c, 7, 0), 0.0)
        for n in range(length):
            c = d * c
            out_ref[strided(length - 1 - n), :] = local[n] + c

    @pl.when(role == 2)
    def _():
        out_ref[strided(0), :] = pltpu.roll(got_ref[strided(length - 1), :], 1, 0)
        for i in range(1, length):
            out_ref[strided(i), :] = got_ref[strided(i - 1), :]

    @pl.when(role == 3)
    def _():
        parts = [got_ref[pl.ds(8 * i, 8), :] for i in range(length)]
        while len(parts) > 1:
            parts = [a + b for a, b in zip(parts[::2], parts[1::2])]
        total = jnp.sum(parts[0], axis=0, keepdims=True) * (1.0 / (COARSEN * SLABS))
        total = jnp.broadcast_to(total, (8, LANES))
        for i in range(length):
            out_ref[pl.ds(8 * i, 8), :] = total


def finish_kernel(got_ref, keep_ref, forward_ref, adjoint_ref, gradient_ref):
    for t in range(TILES):
        cols = pl.ds(t * LANES, LANES)
        forward, scanned, passed, gradient = (got_ref[pl.ds(64 * n + t * ROWS, ROWS), :] for n in range(4))
        forward_ref[:, cols] = forward
        adjoint_ref[:, cols] = scanned + (passed + keep_ref[pl.ds(t * ROWS, ROWS), :])
        gradient_ref[:, cols] = gradient


def in_vmem(count):
    return [pl.BlockSpec(memory_space=pltpu.VMEM)] * count


def in_place(value):
    return pltpu.with_memory_space_constraint(value, pltpu.VMEM)


def field_shape(*lead):
    return pltpu.VMEM((*lead, PHASES, 8, COLS), jnp.float32)


def shards(control, initial, diffusion, reaction, forward_guess, adjoint_guess, observed):
    own = pl.pallas_call(
        pack_kernel,
        out_shape=pltpu.VMEM((7, ROWS, COLS), jnp.float32),
        in_specs=[pl.BlockSpec(memory_space=pl.ANY)] * 7,
        out_specs=in_vmem(1)[0],
        scratch_shapes=[pltpu.SemaphoreType.DMA((7,))],
        name="pack",
    )(control, initial, diffusion, reaction, forward_guess[0], adjoint_guess[0], observed[0])
    other = lax.ppermute(own, "space", [(0, 1), (1, 0)])
    own, other = in_place(own), in_place(other)
    block = jax.ShapeDtypeStruct((ROWS, COLS), jnp.float32)
    rows = pltpu.VMEM((SLABS, LANES), jnp.float32)
    channels, keep = pl.pallas_call(
        relax_kernel,
        out_shape=(rows, pltpu.VMEM((64, LANES), jnp.float32)),
        in_specs=in_vmem(2),
        out_specs=in_vmem(2),
        scratch_shapes=[
            pltpu.VMEM((7, TILES, 2 * ROWS, LANES), jnp.float32),
            field_shape(7),
            field_shape(11),
            field_shape(COARSEN),
            field_shape(COARSEN),
        ],
        name="relax",
    )(own, other)
    got = in_place(lax.all_to_all(channels, TM, 0, 0, tiled=True))
    sent = pl.pallas_call(
        chain_kernel, out_shape=rows, in_specs=in_vmem(2), out_specs=in_vmem(1)[0], name="chain"
    )(got, own)
    back = in_place(lax.all_to_all(sent, TM, 0, 0, tiled=True))
    keep = in_place(keep)
    forward_states, adjoint_states, gradient = pl.pallas_call(
        finish_kernel, out_shape=(block, block, block), in_specs=in_vmem(2), out_specs=in_vmem(3), name="finish"
    )(back, keep)
    return (forward_states[None], adjoint_states[None], gradient)


def solution(mesh):
    finer = Mesh(
        mesh.devices.reshape(2, 8, 8, 2, mesh.shape["space"]),
        ("tm_0", "tm_1", "tm_2", "tm_3", "space"),
    )
    return jax.shard_map(
        shards,
        mesh=finer,
        in_specs=(
            P("space", None),
            P("space", None),
            P("space", None),
            P("space", None),
            P(TM, "space", None),
            P(TM, "space", None),
            P(TM, "space", None),
        ),
        out_specs=(P(TM, "space", None), P(TM, "space", None), P("space", None)),
        check_vma=False,
    )
```

```python
import jax
import jax.numpy as jnp
from jax import lax
from jax.experimental import pallas as pl
from jax.experimental.pallas import tpu as pltpu
from jax.sharding import Mesh
from jax.sharding import PartitionSpec as P

SWEEPS = 3
COARSEN = 8
SLABS = 256
TM = ("tm_0", "tm_1", "tm_2", "tm_3")
ROWS = 16
COLS = 512
LANES = 128
TILES = COLS // LANES
PHASES = 4

ENTRY, FORWARD, ADJOINT, TARGET, CONTROL, SPREAD, REACTION = range(7)
DAMPING, ALPHA, BETA, GAMMA, SOURCE, STATE, TOTAL, FW_LESS, AD_LESS = range(9)


def tm_index():
    return ((lax.axis_index("tm_0") * 8 + lax.axis_index("tm_1")) * 8 + lax.axis_index("tm_2")) * 2 + lax.axis_index(
        "tm_3"
    )


def space_index():
    return lax.axis_index("space")


def each(fn, *fields):
    return [[fn(*cells) for cells in zip(*rows)] for rows in zip(*fields)]


def load(ref, *at):
    return [[ref[(*at, p, t)] for t in range(TILES)] for p in range(PHASES)]


def store(value, ref, *at):
    for p, row in enumerate(value):
        for t, cell in enumerate(row):
            ref[(*at, p, t)] = cell


def trim(field, count):
    return [row[count : len(row) - count] for row in field]


def make_stencil(space):
    sub = lax.broadcasted_iota(jnp.int32, (8, LANES), 0)
    lane = lax.broadcasted_iota(jnp.int32, (8, LANES), 1)
    up_ok = sub != 4 * space
    down_ok = sub != 7 - 4 * space
    first, last = (lane == 0, lane == LANES - 1)

    def widen(field, outside_zero):
        out = []
        for row in field:
            left = [pltpu.roll(cell, 1, 1) for cell in row[TILES - SWEEPS :]]
            right = [pltpu.roll(cell, LANES - 1, 1) for cell in row[:SWEEPS]]
            if outside_zero:
                left = [jnp.where(first, 0.0, cell) for cell in left]
                right = [jnp.where(last, 0.0, cell) for cell in right]
            out.append(left + row + right)
        return out

    def neighbours(field):
        above = [jnp.where(up_ok, pltpu.roll(cell, 1, 0), 0.0) for cell in field[-1][1:-1]]
        below = [jnp.where(down_ok, pltpu.roll(cell, 7, 0), 0.0) for cell in field[0][1:-1]]
        out = []
        for p, row in enumerate(field):
            ups = field[p - 1][1:-1] if p else above
            downs = field[p + 1][1:-1] if p < PHASES - 1 else below
            out.append([(u + d) + (a + b) for u, d, a, b in zip(ups, downs, row[:-2], row[2:])])
        return out

    return widen, neighbours


def exact_terms(value):
    high = value.astype(jnp.bfloat16)
    rest = value - high.astype(jnp.float32)
    middle = rest.astype(jnp.bfloat16)
    low = (rest - middle.astype(jnp.float32)).astype(jnp.bfloat16)
    return high, middle, low


def reorder(value, selection, contracted):
    high, middle, low = (
        lax.dot_general(term, selection, (((1,), (contracted,)), ((), ())), preferred_element_type=jnp.float32)
        for term in exact_terms(value)
    )
    return high + (middle + low)


def pack_kernel(control, initial, diffusion, reaction, forward, adjoint, observed, out_ref, order_ref, raw, sems):
    is_last = tm_index() == SLABS - 1

    def copy(source, slot):
        return pltpu.make_async_copy(source, raw.at[slot], sems.at[slot])

    @pl.when(is_last)
    def _():
        copy(initial, ENTRY).start()

    @pl.when(jnp.logical_not(is_last))
    def _():
        copy(forward, ENTRY).start()

    rest = (
        (forward, FORWARD),
        (adjoint, ADJOINT),
        (observed, TARGET),
        (control, CONTROL),
        (diffusion, SPREAD),
        (reaction, REACTION),
    )
    for source, slot in rest:
        copy(source, slot).start()
    column = lax.broadcasted_iota(jnp.int32, (LANES, COLS), 1)
    lane = lax.broadcasted_iota(jnp.int32, (LANES, COLS), 0)
    for t in range(TILES):
        order_ref[t * LANES : (t + 1) * LANES, :] = jnp.where(column == TILES * lane + t, 1.0, 0.0).astype(jnp.bfloat16)
    copy(forward, ENTRY).wait()
    for source, slot in rest:
        copy(source, slot).wait()
    packed = reorder(raw[...].reshape(7 * ROWS, COLS), order_ref[...], 1)
    out_ref[...] = packed.reshape(7, ROWS, COLS)


def relax_kernel(own_ref, other_ref, chan_ref, keep_ref, raw, grid, field, wide, points, coarse_points):
    slab = tm_index()
    widen, neighbours = make_stencil(space_index())
    is_last = slab == SLABS - 1
    not_last = jnp.where(is_last, 0.0, 1.0)
    not_first = jnp.where(slab == 0, 0.0, 1.0)

    for n in range(7):
        for t in range(TILES):
            cols = pl.ds(t * LANES, LANES)
            raw[n, t, 0:ROWS, :] = own_ref[n, :, cols]
            raw[n, t, ROWS : 2 * ROWS, :] = other_ref[n, :, cols]
    for n in range(7):
        for p in range(PHASES):
            for t in range(TILES):
                grid[n, p, t] = raw[n, t, pl.ds(p, 8, stride=PHASES), :]

    spread, reaction = (load(grid, SPREAD), load(grid, REACTION))
    inverse = each(lambda s, r: 1.0 / (1.0 + 4.0 * s + r), spread, reaction)
    store(widen(inverse, True), wide, 0)
    store(widen(each(jnp.multiply, spread, inverse), True), wide, 1)
    damping = each(lambda r: 1.0 / (1.0 + COARSEN * r), reaction)
    store(damping, field, DAMPING)

    def inverse_wide(count):
        return [[wide[0, p, t] for t in range(SWEEPS - count, SWEEPS + TILES + count)] for p in range(PHASES)]

    def weight_wide(count):
        return [[wide[1, p, t] for t in range(SWEEPS - count, SWEEPS + TILES + count)] for p in range(PHASES)]

    def forward_step(right_side):
        v = widen(right_side, True)
        scaled = each(jnp.multiply, inverse_wide(SWEEPS - 1), trim(v, 1))
        for n in range(SWEEPS):
            v = each(
                lambda s, w, q: s + w * q, trim(scaled, n), weight_wide(SWEEPS - 1 - n), neighbours(v)
            )
        return v

    def adjoint_step(y):
        carried, summed = (widen(y, False), y)
        for n in range(SWEEPS - 1):
            carried = neighbours(each(jnp.multiply, weight_wide(SWEEPS - n), carried))
            summed = each(jnp.add, summed, trim(carried, SWEEPS - 1 - n))
        final = neighbours(each(jnp.multiply, weight_wide(1), carried))
        return each(lambda s, i, f: s * i + f, summed, inverse_wide(0), final)

    store(load(grid, ENTRY), field, STATE)
    store(load(grid, ADJOINT), field, BETA)
    store(each(lambda g: g / COARSEN, load(grid, FORWARD)), field, GAMMA)

    def forward_body(i, _):
        v = forward_step(each(jnp.add, load(field, STATE), load(grid, CONTROL)))
        beta = adjoint_step(load(field, BETA))
        gamma = adjoint_step(each(lambda a, o: a - o / COARSEN, load(field, GAMMA), load(grid, TARGET)))
        store(v, field, STATE)
        store(v, points, i)
        store(beta, field, BETA)
        store(gamma, field, GAMMA)
        return 0

    lax.fori_loop(0, COARSEN, forward_body, 0)

    forward_less = jnp.where(is_last, SLABS - 1, SLABS - 2 - slab)
    adjoint_less = jnp.maximum(slab - 1, 0)
    for slot, count in ((FW_LESS, forward_less), (AD_LESS, adjoint_less)):
        power, block = (damping, each(jnp.ones_like, damping))
        total = each(jnp.zeros_like, damping)
        for b in range(8):
            taken = ((count >> b) & 1) == 1
            total = each(lambda s, v, q: jnp.where(taken, v + q * s, s), total, block, power)
            if b < 7:
                block = each(lambda v, q: v + v * q, block, power)
                power = each(lambda q: q * q, power)
        store(total, field, slot)

    push = each(lambda f, d, g: f - not_last * (d * g), load(field, STATE), load(field, DAMPING), load(grid, FORWARD))
    store(push, field, SOURCE)
    store(
        each(lambda w, u, e: w * u + (1.0 - not_last) * e, load(field, FW_LESS), push, load(grid, ENTRY)),
        field,
        STATE,
    )
    store(each(jnp.zeros_like, push), field, ALPHA)

    def adjoint_body(n, _):
        at = COARSEN - 2 - n
        alpha = adjoint_step(each(lambda a, f: a + f / COARSEN, load(field, ALPHA), load(points, at)))
        v = forward_step(each(jnp.add, load(field, STATE), load(grid, CONTROL)))
        store(alpha, field, ALPHA)
        store(v, field, STATE)
        store(v, coarse_points, n)
        return 0

    lax.fori_loop(0, COARSEN - 1, adjoint_body, 0)

    damping = load(field, DAMPING)
    alpha, beta, gamma = (load(field, ALPHA), load(field, BETA), load(field, GAMMA))
    keep = each(lambda g, d, a: g + not_last * (d * a), gamma, damping, alpha)
    pull = each(lambda k, d, g, b: d * (k - g) + b, keep, damping, load(grid, ADJOINT), beta)
    push = load(field, SOURCE)
    less = load(field, AD_LESS)
    store(
        each(lambda a, k, w, q, d: a + k + not_first * ((1.0 + d * w) * q), alpha, keep, less, pull, damping),
        field,
        TOTAL,
    )
    rest = each(lambda a, k, w, q: not_last * a + not_first * (k + w * q), alpha, keep, less, pull)
    store(
        each(
            lambda t, w, d, u, o: t + ((1.0 + d * w) * u - o) / COARSEN,
            rest,
            load(field, FW_LESS),
            damping,
            push,
            load(grid, TARGET),
        ),
        field,
        GAMMA,
    )
    store(pull, field, BETA)
    store(keep, field, STATE)

    def gradient_body(n, _):
        v = adjoint_step(load(field, GAMMA))
        store(each(jnp.add, load(field, TOTAL), v), field, TOTAL)
        at = COARSEN - 2 - n
        store(
            each(lambda a, f, o: a + (f - o) / COARSEN, v, load(coarse_points, at), load(grid, TARGET)), field, GAMMA
        )
        return 0

    lax.fori_loop(0, COARSEN - 1, gradient_body, 0)

    for n, slot in enumerate((SOURCE, BETA, ALPHA, TOTAL)):
        for p in range(PHASES):
            for t in range(TILES):
                chan_ref[pl.ds((n * TILES + t) * ROWS + p, 4, stride=PHASES), :] = field[slot, p, t, 0:4, :]
    for p in range(PHASES):
        for t in range(TILES):
            keep_ref[pl.ds(t * ROWS + p, 4, stride=PHASES), :] = field[STATE, p, t, 0:4, :]


def chain_kernel(got_ref, own_ref, out_ref):
    owner = tm_index()
    role = owner // 64
    cell = owner % 64
    tile = cell // ROWS
    row = own_ref[REACTION, pl.ds(cell % ROWS, 1), :]
    reaction = row[:, 0:LANES]
    for t in range(1, TILES):
        reaction = jnp.where(tile == t, row[:, t * LANES : (t + 1) * LANES], reaction)
    d = jnp.broadcast_to(1.0 / (1.0 + COARSEN * reaction), (8, LANES))
    length = SLABS // 8
    sub = lax.broadcasted_iota(jnp.int32, (8, LANES), 0)
    d32 = d
    for _ in range(5):
        d32 = d32 * d32
    d64 = d32 * d32
    d128 = d64 * d64

    def strided(i):
        return pl.ds(i, 8, stride=length)

    @pl.when(role == 0)
    def _():
        x = pltpu.roll(got_ref[strided(length - 1), :], 1, 0)
        local = [x]
        for i in range(1, length):
            x = d * x + got_ref[strided(i - 1), :]
            local.append(x)
        c = x
        c = c + jnp.where(sub >= 1, d32 * pltpu.roll(c, 1, 0), 0.0)
        c = c + jnp.where(sub >= 2, d64 * pltpu.roll(c, 2, 0), 0.0)
        c = c + jnp.where(sub >= 4, d128 * pltpu.roll(c, 4, 0), 0.0)
        c = jnp.where(sub >= 1, pltpu.roll(c, 1, 0), 0.0)
        for i in range(length):
            c = d * c
            out_ref[strided(i), :] = local[i] + c

    @pl.when(role == 1)
    def _():
        x = jnp.where(sub == 7, 0.0, pltpu.roll(got_ref[strided(0), :], 7, 0))
        local = [x]
        for i in range(length - 2, -1, -1):
            x = d * x + got_ref[strided(i + 1), :]
            local.append(x)
        c = x
        c = c + jnp.where(sub < 7, d32 * pltpu.roll(c, 7, 0), 0.0)
        c = c + jnp.where(sub < 6, d64 * pltpu.roll(c, 6, 0), 0.0)
        c = c + jnp.where(sub < 4, d128 * pltpu.roll(c, 4, 0), 0.0)
        c = jnp.where(sub < 7, pltpu.roll(c, 7, 0), 0.0)
        for n in range(length):
            c = d * c
            out_ref[strided(length - 1 - n), :] = local[n] + c

    @pl.when(role == 2)
    def _():
        out_ref[strided(0), :] = pltpu.roll(got_ref[strided(length - 1), :], 1, 0)
        for i in range(1, length):
            out_ref[strided(i), :] = got_ref[strided(i - 1), :]

    @pl.when(role == 3)
    def _():
        parts = [got_ref[pl.ds(8 * i, 8), :] for i in range(length)]
        while len(parts) > 1:
            parts = [a + b for a, b in zip(parts[::2], parts[1::2])]
        total = jnp.sum(parts[0], axis=0, keepdims=True) * (1.0 / (COARSEN * SLABS))
        total = jnp.broadcast_to(total, (8, LANES))
        for i in range(length):
            out_ref[pl.ds(8 * i, 8), :] = total


def finish_kernel(got_ref, keep_ref, order_ref, forward_ref, adjoint_ref, gradient_ref):
    def rows(ref, n):
        return jnp.concatenate([ref[pl.ds((n * TILES + t) * ROWS, ROWS), :] for t in range(TILES)], 1)

    adjoint = rows(got_ref, 1) + (rows(got_ref, 2) + rows(keep_ref, 0))
    parts = jnp.concatenate([rows(got_ref, 0), adjoint, rows(got_ref, 3)], 0)
    parts = reorder(parts, order_ref[...], 0)
    forward_ref[...] = parts[0:ROWS]
    adjoint_ref[...] = parts[ROWS : 2 * ROWS]
    gradient_ref[...] = parts[2 * ROWS : 3 * ROWS]


def in_vmem(count):
    return [pl.BlockSpec(memory_space=pltpu.VMEM)] * count


def in_place(value):
    return pltpu.with_memory_space_constraint(value, pltpu.VMEM)


def field_shape(*lead):
    return pltpu.VMEM((*lead, PHASES, TILES, 8, LANES), jnp.float32)


def relax_scratch():
    return [
        pltpu.VMEM((7, TILES, 2 * ROWS, LANES), jnp.float32),
        field_shape(7),
        field_shape(9),
        pltpu.VMEM((2, PHASES, TILES + 2 * SWEEPS, 8, LANES), jnp.float32),
        field_shape(COARSEN),
        field_shape(COARSEN - 1),
    ]


def shards(control, initial, diffusion, reaction, forward_guess, adjoint_guess, observed):
    own, order = pl.pallas_call(
        pack_kernel,
        out_shape=(pltpu.VMEM((7, ROWS, COLS), jnp.float32), pltpu.VMEM((COLS, COLS), jnp.bfloat16)),
        in_specs=[pl.BlockSpec(memory_space=pl.ANY)] * 7,
        out_specs=in_vmem(2),
        scratch_shapes=[pltpu.VMEM((7, ROWS, COLS), jnp.float32), pltpu.SemaphoreType.DMA((7,))],
        name="pack",
    )(control, initial, diffusion, reaction, forward_guess[0], adjoint_guess[0], observed[0])
    other = lax.ppermute(own, "space", [(0, 1), (1, 0)])
    own, other = in_place(own), in_place(other)
    block = jax.ShapeDtypeStruct((ROWS, COLS), jnp.float32)
    rows = pltpu.VMEM((SLABS, LANES), jnp.float32)
    channels, keep = pl.pallas_call(
        relax_kernel,
        out_shape=(rows, pltpu.VMEM((64, LANES), jnp.float32)),
        in_specs=in_vmem(2),
        out_specs=in_vmem(2),
        scratch_shapes=relax_scratch(),
        name="relax",
    )(own, other)
    got = in_place(lax.all_to_all(channels, TM, 0, 0, tiled=True))
    sent = pl.pallas_call(
        chain_kernel, out_shape=rows, in_specs=in_vmem(2), out_specs=in_vmem(1)[0], name="chain"
    )(got, own)
    back = in_place(lax.all_to_all(sent, TM, 0, 0, tiled=True))
    keep, order = in_place(keep), in_place(order)
    forward_states, adjoint_states, gradient = pl.pallas_call(
        finish_kernel, out_shape=(block, block, block), in_specs=in_vmem(3), out_specs=in_vmem(3), name="finish"
    )(back, keep, order)
    return (forward_states[None], adjoint_states[None], gradient)


def solution(mesh):
    finer = Mesh(
        mesh.devices.reshape(2, 8, 8, 2, mesh.shape["space"]),
        ("tm_0", "tm_1", "tm_2", "tm_3", "space"),
    )
    return jax.shard_map(
        shards,
        mesh=finer,
        in_specs=(
            P("space", None),
            P("space", None),
            P("space", None),
            P("space", None),
            P(TM, "space", None),
            P(TM, "space", None),
            P(TM, "space", None),
        ),
        out_specs=(P(TM, "space", None), P(TM, "space", None), P("space", None)),
        check_vma=False,
    )
```

```python
import jax
import jax.numpy as jnp
from jax import lax
from jax.experimental import pallas as pl
from jax.experimental.pallas import tpu as pltpu
from jax.sharding import Mesh
from jax.sharding import PartitionSpec as P

SWEEPS = 3
COARSEN = 8
SLABS = 256
TM = ("tm_0", "tm_1", "tm_2", "tm_3")
ROWS = 16
COLS = 512
LANES = 128
TILES = COLS // LANES
PHASES = 4

ENTRY, FORWARD, ADJOINT, TARGET, CONTROL, SPREAD, REACTION = range(7)
DAMPING, ALPHA, BETA, GAMMA, SOURCE, STATE, TOTAL, FW_LESS, AD_LESS = range(9)


def tm_index():
    return ((lax.axis_index("tm_0") * 8 + lax.axis_index("tm_1")) * 8 + lax.axis_index("tm_2")) * 2 + lax.axis_index(
        "tm_3"
    )


def space_index():
    return lax.axis_index("space")


def each(fn, *fields):
    return [[fn(*cells) for cells in zip(*rows)] for rows in zip(*fields)]


def load(ref, *at):
    return [[ref[(*at, p, t)] for t in range(TILES)] for p in range(PHASES)]


def store(value, ref, *at):
    for p, row in enumerate(value):
        for t, cell in enumerate(row):
            ref[(*at, p, t)] = cell


def trim(field, count):
    return [row[count : len(row) - count] for row in field]


def make_stencil(space):
    sub = lax.broadcasted_iota(jnp.int32, (8, LANES), 0)
    lane = lax.broadcasted_iota(jnp.int32, (8, LANES), 1)
    up_ok = sub != 4 * space
    down_ok = sub != 7 - 4 * space
    first, last = (lane == 0, lane == LANES - 1)

    def widen(field, outside_zero):
        out = []
        for row in field:
            left = [pltpu.roll(cell, 1, 1) for cell in row[TILES - SWEEPS :]]
            right = [pltpu.roll(cell, LANES - 1, 1) for cell in row[:SWEEPS]]
            if outside_zero:
                left = [jnp.where(first, 0.0, cell) for cell in left]
                right = [jnp.where(last, 0.0, cell) for cell in right]
            out.append(left + row + right)
        return out

    def neighbours(field):
        above = [jnp.where(up_ok, pltpu.roll(cell, 1, 0), 0.0) for cell in field[-1][1:-1]]
        below = [jnp.where(down_ok, pltpu.roll(cell, 7, 0), 0.0) for cell in field[0][1:-1]]
        out = []
        for p, row in enumerate(field):
            ups = field[p - 1][1:-1] if p else above
            downs = field[p + 1][1:-1] if p < PHASES - 1 else below
            out.append([(u + d) + (a + b) for u, d, a, b in zip(ups, downs, row[:-2], row[2:])])
        return out

    return widen, neighbours


def exact_terms(value):
    high = value.astype(jnp.bfloat16)
    rest = value - high.astype(jnp.float32)
    middle = rest.astype(jnp.bfloat16)
    low = (rest - middle.astype(jnp.float32)).astype(jnp.bfloat16)
    return high, middle, low


def reorder(value, selection, contracted):
    high, middle, low = (
        lax.dot_general(term, selection, (((1,), (contracted,)), ((), ())), preferred_element_type=jnp.float32)
        for term in exact_terms(value)
    )
    return high + (middle + low)


def pack_kernel(control, initial, diffusion, reaction, forward, adjoint, observed, out_ref, order_ref, raw, sems):
    is_last = tm_index() == SLABS - 1

    def copy(source, slot):
        return pltpu.make_async_copy(source, raw.at[slot], sems.at[slot])

    @pl.when(is_last)
    def _():
        copy(initial, ENTRY).start()

    @pl.when(jnp.logical_not(is_last))
    def _():
        copy(forward, ENTRY).start()

    rest = (
        (forward, FORWARD),
        (adjoint, ADJOINT),
        (observed, TARGET),
        (control, CONTROL),
        (diffusion, SPREAD),
        (reaction, REACTION),
    )
    for source, slot in rest:
        copy(source, slot).start()
    column = lax.broadcasted_iota(jnp.int32, (LANES, COLS), 1)
    lane = lax.broadcasted_iota(jnp.int32, (LANES, COLS), 0)
    for t in range(TILES):
        order_ref[t * LANES : (t + 1) * LANES, :] = jnp.where(column == TILES * lane + t, 1.0, 0.0).astype(jnp.bfloat16)
    copy(forward, ENTRY).wait()
    for source, slot in rest:
        copy(source, slot).wait()
    packed = reorder(raw[...].reshape(7 * ROWS, COLS), order_ref[...], 1)
    out_ref[...] = packed.reshape(7, ROWS, COLS)


def relax_kernel(own_ref, both_ref, chan_ref, keep_ref, raw, grid, field, wide, points, coarse_points):
    slab = tm_index()
    space = space_index()
    widen, neighbours = make_stencil(space)
    is_last = slab == SLABS - 1
    not_last = jnp.where(is_last, 0.0, 1.0)
    not_first = jnp.where(slab == 0, 0.0, 1.0)

    for n in range(7):
        for t in range(TILES):
            cols = pl.ds(t * LANES, LANES)
            raw[n, t, 0:ROWS, :] = own_ref[n, :, cols]
            raw[n, t, ROWS : 2 * ROWS, :] = both_ref[1 - space, n, :, cols]
    for n in range(7):
        for p in range(PHASES):
            for t in range(TILES):
                grid[n, p, t] = raw[n, t, pl.ds(p, 8, stride=PHASES), :]

    spread, reaction = (load(grid, SPREAD), load(grid, REACTION))
    inverse = each(lambda s, r: 1.0 / (1.0 + 4.0 * s + r), spread, reaction)
    store(widen(inverse, True), wide, 0)
    store(widen(each(jnp.multiply, spread, inverse), True), wide, 1)
    damping = each(lambda r: 1.0 / (1.0 + COARSEN * r), reaction)
    store(damping, field, DAMPING)

    def inverse_wide(count):
        return [[wide[0, p, t] for t in range(SWEEPS - count, SWEEPS + TILES + count)] for p in range(PHASES)]

    def weight_wide(count):
        return [[wide[1, p, t] for t in range(SWEEPS - count, SWEEPS + TILES + count)] for p in range(PHASES)]

    def forward_step(right_side):
        v = widen(right_side, True)
        scaled = each(jnp.multiply, inverse_wide(SWEEPS - 1), trim(v, 1))
        for n in range(SWEEPS):
            v = each(
                lambda s, w, q: s + w * q, trim(scaled, n), weight_wide(SWEEPS - 1 - n), neighbours(v)
            )
        return v

    def adjoint_step(y):
        carried, summed = (widen(y, False), y)
        for n in range(SWEEPS - 1):
            carried = neighbours(each(jnp.multiply, weight_wide(SWEEPS - n), carried))
            summed = each(jnp.add, summed, trim(carried, SWEEPS - 1 - n))
        final = neighbours(each(jnp.multiply, weight_wide(1), carried))
        return each(lambda s, i, f: s * i + f, summed, inverse_wide(0), final)

    store(load(grid, ENTRY), field, STATE)
    store(load(grid, ADJOINT), field, BETA)
    store(each(lambda g: g / COARSEN, load(grid, FORWARD)), field, GAMMA)

    def forward_body(i, _):
        v = forward_step(each(jnp.add, load(field, STATE), load(grid, CONTROL)))
        beta = adjoint_step(load(field, BETA))
        gamma = adjoint_step(each(lambda a, o: a - o / COARSEN, load(field, GAMMA), load(grid, TARGET)))
        store(v, field, STATE)
        store(v, points, i)
        store(beta, field, BETA)
        store(gamma, field, GAMMA)
        return 0

    lax.fori_loop(0, COARSEN, forward_body, 0)

    forward_less = jnp.where(is_last, SLABS - 1, SLABS - 2 - slab)
    adjoint_less = jnp.maximum(slab - 1, 0)
    for slot, count in ((FW_LESS, forward_less), (AD_LESS, adjoint_less)):
        power, block = (damping, each(jnp.ones_like, damping))
        total = each(jnp.zeros_like, damping)
        for b in range(8):
            taken = ((count >> b) & 1) == 1
            total = each(lambda s, v, q: jnp.where(taken, v + q * s, s), total, block, power)
            if b < 7:
                block = each(lambda v, q: v + v * q, block, power)
                power = each(lambda q: q * q, power)
        store(total, field, slot)

    push = each(lambda f, d, g: f - not_last * (d * g), load(field, STATE), load(field, DAMPING), load(grid, FORWARD))
    store(push, field, SOURCE)
    store(
        each(lambda w, u, e: w * u + (1.0 - not_last) * e, load(field, FW_LESS), push, load(grid, ENTRY)),
        field,
        STATE,
    )
    store(each(jnp.zeros_like, push), field, ALPHA)

    def adjoint_body(n, _):
        at = COARSEN - 2 - n
        alpha = adjoint_step(each(lambda a, f: a + f / COARSEN, load(field, ALPHA), load(points, at)))
        v = forward_step(each(jnp.add, load(field, STATE), load(grid, CONTROL)))
        store(alpha, field, ALPHA)
        store(v, field, STATE)
        store(v, coarse_points, n)
        return 0

    lax.fori_loop(0, COARSEN - 1, adjoint_body, 0)

    damping = load(field, DAMPING)
    alpha, beta, gamma = (load(field, ALPHA), load(field, BETA), load(field, GAMMA))
    keep = each(lambda g, d, a: g + not_last * (d * a), gamma, damping, alpha)
    pull = each(lambda k, d, g, b: d * (k - g) + b, keep, damping, load(grid, ADJOINT), beta)
    push = load(field, SOURCE)
    less = load(field, AD_LESS)
    store(
        each(lambda a, k, w, q, d: a + k + not_first * ((1.0 + d * w) * q), alpha, keep, less, pull, damping),
        field,
        TOTAL,
    )
    rest = each(lambda a, k, w, q: not_last * a + not_first * (k + w * q), alpha, keep, less, pull)
    store(
        each(
            lambda t, w, d, u, o: t + ((1.0 + d * w) * u - o) / COARSEN,
            rest,
            load(field, FW_LESS),
            damping,
            push,
            load(grid, TARGET),
        ),
        field,
        GAMMA,
    )
    store(pull, field, BETA)
    store(keep, field, STATE)

    def gradient_body(n, _):
        v = adjoint_step(load(field, GAMMA))
        store(each(jnp.add, load(field, TOTAL), v), field, TOTAL)
        at = COARSEN - 2 - n
        store(
            each(lambda a, f, o: a + (f - o) / COARSEN, v, load(coarse_points, at), load(grid, TARGET)), field, GAMMA
        )
        return 0

    lax.fori_loop(0, COARSEN - 1, gradient_body, 0)

    for n, slot in enumerate((SOURCE, BETA, ALPHA, TOTAL)):
        for p in range(PHASES):
            for t in range(TILES):
                chan_ref[pl.ds((n * TILES + t) * ROWS + p, 4, stride=PHASES), :] = field[slot, p, t, 0:4, :]
    for p in range(PHASES):
        for t in range(TILES):
            keep_ref[pl.ds(t * ROWS + p, 4, stride=PHASES), :] = field[STATE, p, t, 0:4, :]


def chain_kernel(got_ref, own_ref, out_ref):
    owner = tm_index()
    role = owner // 64
    cell = owner % 64
    tile = cell // ROWS
    row = own_ref[REACTION, pl.ds(cell % ROWS, 1), :]
    reaction = row[:, 0:LANES]
    for t in range(1, TILES):
        reaction = jnp.where(tile == t, row[:, t * LANES : (t + 1) * LANES], reaction)
    d = jnp.broadcast_to(1.0 / (1.0 + COARSEN * reaction), (8, LANES))
    length = SLABS // 8
    sub = lax.broadcasted_iota(jnp.int32, (8, LANES), 0)
    d32 = d
    for _ in range(5):
        d32 = d32 * d32
    d64 = d32 * d32
    d128 = d64 * d64

    def strided(i):
        return pl.ds(i, 8, stride=length)

    @pl.when(role == 0)
    def _():
        x = pltpu.roll(got_ref[strided(length - 1), :], 1, 0)
        local = [x]
        for i in range(1, length):
            x = d * x + got_ref[strided(i - 1), :]
            local.append(x)
        c = x
        c = c + jnp.where(sub >= 1, d32 * pltpu.roll(c, 1, 0), 0.0)
        c = c + jnp.where(sub >= 2, d64 * pltpu.roll(c, 2, 0), 0.0)
        c = c + jnp.where(sub >= 4, d128 * pltpu.roll(c, 4, 0), 0.0)
        c = jnp.where(sub >= 1, pltpu.roll(c, 1, 0), 0.0)
        for i in range(length):
            c = d * c
            out_ref[strided(i), :] = local[i] + c

    @pl.when(role == 1)
    def _():
        x = jnp.where(sub == 7, 0.0, pltpu.roll(got_ref[strided(0), :], 7, 0))
        local = [x]
        for i in range(length - 2, -1, -1):
            x = d * x + got_ref[strided(i + 1), :]
            local.append(x)
        c = x
        c = c + jnp.where(sub < 7, d32 * pltpu.roll(c, 7, 0), 0.0)
        c = c + jnp.where(sub < 6, d64 * pltpu.roll(c, 6, 0), 0.0)
        c = c + jnp.where(sub < 4, d128 * pltpu.roll(c, 4, 0), 0.0)
        c = jnp.where(sub < 7, pltpu.roll(c, 7, 0), 0.0)
        for n in range(length):
            c = d * c
            out_ref[strided(length - 1 - n), :] = local[n] + c

    @pl.when(role == 2)
    def _():
        out_ref[strided(0), :] = pltpu.roll(got_ref[strided(length - 1), :], 1, 0)
        for i in range(1, length):
            out_ref[strided(i), :] = got_ref[strided(i - 1), :]

    @pl.when(role == 3)
    def _():
        parts = [got_ref[pl.ds(8 * i, 8), :] for i in range(length)]
        while len(parts) > 1:
            parts = [a + b for a, b in zip(parts[::2], parts[1::2])]
        total = jnp.sum(parts[0], axis=0, keepdims=True) * (1.0 / (COARSEN * SLABS))
        total = jnp.broadcast_to(total, (8, LANES))
        for i in range(length):
            out_ref[pl.ds(8 * i, 8), :] = total


def finish_kernel(got_ref, keep_ref, order_ref, forward_ref, adjoint_ref, gradient_ref):
    def rows(ref, n):
        return jnp.concatenate([ref[pl.ds((n * TILES + t) * ROWS, ROWS), :] for t in range(TILES)], 1)

    adjoint = rows(got_ref, 1) + (rows(got_ref, 2) + rows(keep_ref, 0))
    parts = jnp.concatenate([rows(got_ref, 0), adjoint, rows(got_ref, 3)], 0)
    parts = reorder(parts, order_ref[...], 0)
    forward_ref[...] = parts[0:ROWS]
    adjoint_ref[...] = parts[ROWS : 2 * ROWS]
    gradient_ref[...] = parts[2 * ROWS : 3 * ROWS]


def in_vmem(count):
    return [pl.BlockSpec(memory_space=pltpu.VMEM)] * count


def in_place(value):
    return pltpu.with_memory_space_constraint(value, pltpu.VMEM)


def field_shape(*lead):
    return pltpu.VMEM((*lead, PHASES, TILES, 8, LANES), jnp.float32)


def relax_scratch():
    return [
        pltpu.VMEM((7, TILES, 2 * ROWS, LANES), jnp.float32),
        field_shape(7),
        field_shape(9),
        pltpu.VMEM((2, PHASES, TILES + 2 * SWEEPS, 8, LANES), jnp.float32),
        field_shape(COARSEN),
        field_shape(COARSEN - 1),
    ]


def shards(control, initial, diffusion, reaction, forward_guess, adjoint_guess, observed):
    own, order = pl.pallas_call(
        pack_kernel,
        out_shape=(pltpu.VMEM((7, ROWS, COLS), jnp.float32), pltpu.VMEM((COLS, COLS), jnp.bfloat16)),
        in_specs=[pl.BlockSpec(memory_space=pl.ANY)] * 7,
        out_specs=in_vmem(2),
        scratch_shapes=[pltpu.VMEM((7, ROWS, COLS), jnp.float32), pltpu.SemaphoreType.DMA((7,))],
        name="pack",
    )(control, initial, diffusion, reaction, forward_guess[0], adjoint_guess[0], observed[0])
    both = in_place(lax.all_gather(own, "space", axis=0))
    own = in_place(own)
    block = jax.ShapeDtypeStruct((ROWS, COLS), jnp.float32)
    rows = pltpu.VMEM((SLABS, LANES), jnp.float32)
    channels, keep = pl.pallas_call(
        relax_kernel,
        out_shape=(rows, pltpu.VMEM((64, LANES), jnp.float32)),
        in_specs=in_vmem(2),
        out_specs=in_vmem(2),
        scratch_shapes=relax_scratch(),
        name="relax",
    )(own, both)
    got = in_place(lax.all_to_all(channels, TM, 0, 0, tiled=True))
    sent = pl.pallas_call(
        chain_kernel, out_shape=rows, in_specs=in_vmem(2), out_specs=in_vmem(1)[0], name="chain"
    )(got, own)
    back = in_place(lax.all_to_all(sent, TM, 0, 0, tiled=True))
    keep, order = in_place(keep), in_place(order)
    forward_states, adjoint_states, gradient = pl.pallas_call(
        finish_kernel, out_shape=(block, block, block), in_specs=in_vmem(3), out_specs=in_vmem(3), name="finish"
    )(back, keep, order)
    return (forward_states[None], adjoint_states[None], gradient)


def solution(mesh):
    finer = Mesh(
        mesh.devices.reshape(2, 8, 8, 2, mesh.shape["space"]),
        ("tm_0", "tm_1", "tm_2", "tm_3", "space"),
    )
    return jax.shard_map(
        shards,
        mesh=finer,
        in_specs=(
            P("space", None),
            P("space", None),
            P("space", None),
            P("space", None),
            P(TM, "space", None),
            P(TM, "space", None),
            P(TM, "space", None),
        ),
        out_specs=(P(TM, "space", None), P(TM, "space", None), P("space", None)),
        check_vma=False,
    )
```

```python
import jax
import jax.numpy as jnp
from jax import lax
from jax.experimental import pallas as pl
from jax.experimental.pallas import tpu as pltpu
from jax.sharding import Mesh
from jax.sharding import PartitionSpec as P

SWEEPS = 3
COARSEN = 8
SLABS = 256
TM = ("tm_0", "tm_1", "tm_2", "tm_3")
ROWS = 16
COLS = 512
LANES = 128
TILES = COLS // LANES
PHASES = 4
BLOCK = 16
BLOCKS = SLABS // BLOCK

ENTRY, FORWARD, ADJOINT, TARGET, CONTROL, SPREAD, REACTION = range(7)
DAMPING, ALPHA, BETA, GAMMA, SOURCE, STATE, TOTAL, FW_LESS, AD_LESS = range(9)


def tm_index():
    return ((lax.axis_index("tm_0") * 8 + lax.axis_index("tm_1")) * 8 + lax.axis_index("tm_2")) * 2 + lax.axis_index(
        "tm_3"
    )


def space_index():
    return lax.axis_index("space")


def each(fn, *fields):
    return [[fn(*cells) for cells in zip(*rows)] for rows in zip(*fields)]


def load(ref, *at):
    return [[ref[(*at, p, t)] for t in range(TILES)] for p in range(PHASES)]


def store(value, ref, *at):
    for p, row in enumerate(value):
        for t, cell in enumerate(row):
            ref[(*at, p, t)] = cell


def trim(field, count):
    return [row[count : len(row) - count] for row in field]


def make_stencil(space):
    sub = lax.broadcasted_iota(jnp.int32, (8, LANES), 0)
    lane = lax.broadcasted_iota(jnp.int32, (8, LANES), 1)
    up_ok = sub != 4 * space
    down_ok = sub != 7 - 4 * space
    first, last = (lane == 0, lane == LANES - 1)

    def widen(field, outside_zero):
        out = []
        for row in field:
            left = [pltpu.roll(cell, 1, 1) for cell in row[TILES - SWEEPS :]]
            right = [pltpu.roll(cell, LANES - 1, 1) for cell in row[:SWEEPS]]
            if outside_zero:
                left = [jnp.where(first, 0.0, cell) for cell in left]
                right = [jnp.where(last, 0.0, cell) for cell in right]
            out.append(left + row + right)
        return out

    def neighbours(field):
        above = [jnp.where(up_ok, pltpu.roll(cell, 1, 0), 0.0) for cell in field[-1][1:-1]]
        below = [jnp.where(down_ok, pltpu.roll(cell, 7, 0), 0.0) for cell in field[0][1:-1]]
        out = []
        pairs = [[u + a for u, a in zip(above, field[0][:-2])]]
        for p in range(1, PHASES):
            pairs.append([u + a for u, a in zip(field[p - 1][1:], field[p][:-1])])
        pairs.append([b + d for b, d in zip(field[-1][2:], below)])
        for p in range(PHASES):
            upper = pairs[p][:-1] if p else pairs[p]
            lower = pairs[p + 1][1:] if p < PHASES - 1 else pairs[p + 1]
            out.append([x + y for x, y in zip(upper, lower)])
        return out

    return widen, neighbours


def exact_terms(value):
    high = value.astype(jnp.bfloat16)
    rest = value - high.astype(jnp.float32)
    middle = rest.astype(jnp.bfloat16)
    low = (rest - middle.astype(jnp.float32)).astype(jnp.bfloat16)
    return high, middle, low


def reorder(value, selection):
    high, middle, low = (
        jnp.dot(term, selection, preferred_element_type=jnp.float32)
        for term in exact_terms(value)
    )
    return high + (middle + low)


def pack_kernel(control, initial, diffusion, reaction, forward, adjoint, observed, out_ref, order_ref, raw, into, sems):
    is_last = tm_index() == SLABS - 1

    def copy(source, slot):
        return pltpu.make_async_copy(source, raw.at[slot], sems.at[slot])

    @pl.when(is_last)
    def _():
        copy(initial, ENTRY).start()

    @pl.when(jnp.logical_not(is_last))
    def _():
        copy(forward, ENTRY).start()

    rest = (
        (forward, FORWARD),
        (adjoint, ADJOINT),
        (observed, TARGET),
        (control, CONTROL),
        (diffusion, SPREAD),
        (reaction, REACTION),
    )
    for source, slot in rest:
        copy(source, slot).start()
    column, lane = (lax.broadcasted_iota(jnp.int32, (LANES, COLS), d) for d in (1, 0))
    for t in range(TILES):
        order_ref[t * LANES : (t + 1) * LANES, :] = jnp.where(column == TILES * lane + t, 1.0, 0.0).astype(jnp.bfloat16)
    column, lane = (lax.broadcasted_iota(jnp.int32, (COLS, LANES), d) for d in (0, 1))
    for t in range(TILES):
        into[:, t * LANES : (t + 1) * LANES] = jnp.where(column == TILES * lane + t, 1.0, 0.0).astype(jnp.bfloat16)
    copy(forward, ENTRY).wait()
    for source, slot in rest:
        copy(source, slot).wait()
    packed = reorder(raw[...].reshape(7 * ROWS, COLS), into[...])
    out_ref[...] = packed.reshape(7, ROWS, COLS)


def relax_kernel(own_ref, both_ref, chan_ref, keep_ref, raw, grid, field, wide, points, coarse_points):
    slab = tm_index()
    space = space_index()
    widen, neighbours = make_stencil(space)
    is_last = slab == SLABS - 1
    not_last = jnp.where(is_last, 0.0, 1.0)
    not_first = jnp.where(slab == 0, 0.0, 1.0)

    for n in range(7):
        for t in range(TILES):
            cols = pl.ds(t * LANES, LANES)
            raw[n, t, 0:ROWS, :] = own_ref[n, :, cols]
            raw[n, t, ROWS : 2 * ROWS, :] = both_ref[1 - space, n, :, cols]
    for n in range(7):
        for p in range(PHASES):
            for t in range(TILES):
                grid[n, p, t] = raw[n, t, pl.ds(p, 8, stride=PHASES), :]

    spread, reaction = (load(grid, SPREAD), load(grid, REACTION))
    inverse = each(lambda s, r: 1.0 / (1.0 + 4.0 * s + r), spread, reaction)
    store(widen(inverse, True), wide, 0)
    store(widen(each(jnp.multiply, spread, inverse), True), wide, 1)
    damping = each(lambda r: 1.0 / (1.0 + COARSEN * r), reaction)
    store(damping, field, DAMPING)

    def inverse_wide(count):
        return [[wide[0, p, t] for t in range(SWEEPS - count, SWEEPS + TILES + count)] for p in range(PHASES)]

    def weight_wide(count):
        return [[wide[1, p, t] for t in range(SWEEPS - count, SWEEPS + TILES + count)] for p in range(PHASES)]

    def forward_step(right_side):
        v = widen(right_side, True)
        scaled = each(jnp.multiply, inverse_wide(SWEEPS - 1), trim(v, 1))
        for n in range(SWEEPS):
            v = each(
                lambda s, w, q: s + w * q, trim(scaled, n), weight_wide(SWEEPS - 1 - n), neighbours(v)
            )
        return v

    def adjoint_step(y):
        carried, summed = (widen(y, False), y)
        for n in range(SWEEPS - 1):
            carried = neighbours(each(jnp.multiply, weight_wide(SWEEPS - n), carried))
            summed = each(jnp.add, summed, trim(carried, SWEEPS - 1 - n))
        final = neighbours(each(jnp.multiply, weight_wide(1), carried))
        return each(lambda s, i, f: s * i + f, summed, inverse_wide(0), final)

    store(load(grid, ENTRY), field, STATE)
    store(load(grid, ADJOINT), field, BETA)
    store(each(lambda g: g / COARSEN, load(grid, FORWARD)), field, GAMMA)

    def forward_body(i, _):
        v = forward_step(each(jnp.add, load(field, STATE), load(grid, CONTROL)))
        beta = adjoint_step(load(field, BETA))
        gamma = adjoint_step(each(lambda a, o: a - o / COARSEN, load(field, GAMMA), load(grid, TARGET)))
        store(v, field, STATE)
        store(v, points, i)
        store(beta, field, BETA)
        store(gamma, field, GAMMA)
        return 0

    lax.fori_loop(0, COARSEN, forward_body, 0)

    forward_less = jnp.where(is_last, SLABS - 1, SLABS - 2 - slab)
    adjoint_less = jnp.maximum(slab - 1, 0)
    for slot, count in ((FW_LESS, forward_less), (AD_LESS, adjoint_less)):
        power, block = (damping, each(jnp.ones_like, damping))
        total = each(jnp.zeros_like, damping)
        for b in range(8):
            taken = ((count >> b) & 1) == 1
            total = each(lambda s, v, q: jnp.where(taken, v + q * s, s), total, block, power)
            if b < 7:
                block = each(lambda v, q: v + v * q, block, power)
                power = each(lambda q: q * q, power)
        store(total, field, slot)

    push = each(lambda f, d, g: f - not_last * (d * g), load(field, STATE), load(field, DAMPING), load(grid, FORWARD))
    store(push, field, SOURCE)
    store(
        each(lambda w, u, e: w * u + (1.0 - not_last) * e, load(field, FW_LESS), push, load(grid, ENTRY)),
        field,
        STATE,
    )
    store(each(jnp.zeros_like, push), field, ALPHA)

    def adjoint_body(n, _):
        at = COARSEN - 2 - n
        alpha = adjoint_step(each(lambda a, f: a + f / COARSEN, load(field, ALPHA), load(points, at)))
        v = forward_step(each(jnp.add, load(field, STATE), load(grid, CONTROL)))
        store(alpha, field, ALPHA)
        store(v, field, STATE)
        store(v, coarse_points, n)
        return 0

    lax.fori_loop(0, COARSEN - 1, adjoint_body, 0, unroll=True)

    damping = load(field, DAMPING)
    alpha, beta, gamma = (load(field, ALPHA), load(field, BETA), load(field, GAMMA))
    keep = each(lambda g, d, a: g + not_last * (d * a), gamma, damping, alpha)
    pull = each(lambda k, d, g, b: d * (k - g) + b, keep, damping, load(grid, ADJOINT), beta)
    push = load(field, SOURCE)
    less = load(field, AD_LESS)
    store(
        each(lambda a, k, w, q, d: a + k + not_first * ((1.0 + d * w) * q), alpha, keep, less, pull, damping),
        field,
        TOTAL,
    )
    rest = each(lambda a, k, w, q: not_last * a + not_first * (k + w * q), alpha, keep, less, pull)
    store(
        each(
            lambda t, w, d, u, o: t + ((1.0 + d * w) * u - o) / COARSEN,
            rest,
            load(field, FW_LESS),
            damping,
            push,
            load(grid, TARGET),
        ),
        field,
        GAMMA,
    )
    store(pull, field, BETA)
    store(keep, field, STATE)

    def gradient_body(n, _):
        v = adjoint_step(load(field, GAMMA))
        store(each(jnp.add, load(field, TOTAL), v), field, TOTAL)
        at = COARSEN - 2 - n
        store(
            each(lambda a, f, o: a + (f - o) / COARSEN, v, load(coarse_points, at), load(grid, TARGET)), field, GAMMA
        )
        return 0

    lax.fori_loop(0, COARSEN - 1, gradient_body, 0, unroll=True)

    for n, slot in enumerate((SOURCE, BETA, ALPHA, TOTAL)):
        for p in range(PHASES):
            for t in range(TILES):
                raw[n, t, pl.ds(p, 4, stride=PHASES), :] = field[slot, p, t, 0:4, :]
    for n in range(4):
        for t in range(TILES):
            for h in range(2):
                chan_ref[2 * t + h, n] = raw[n, t, 8 * h : 8 * h + 8, :]
    for p in range(PHASES):
        for t in range(TILES):
            keep_ref[pl.ds(t * ROWS + p, 4, stride=PHASES), :] = field[STATE, p, t, 0:4, :]


def owned_damping(own_ref):
    owner = lax.axis_index("tm_2")
    rows = own_ref[REACTION, pl.ds(pl.multiple_of(8 * (owner % 2), 8), 8), :]
    reaction = rows[:, 0:LANES]
    for t in range(1, TILES):
        reaction = jnp.where(owner // 2 == t, rows[:, t * LANES : (t + 1) * LANES], reaction)
    return 1.0 / (1.0 + COARSEN * reaction)


def block_kernel(got_ref, own_ref, totals_ref, local_ref):
    d = owned_damping(own_ref)
    block = lax.axis_index("tm_0") * 8 + lax.axis_index("tm_1")
    even = lax.axis_index("tm_3") == 0

    def source(n, i):
        return got_ref[i % 2, i // 2, n]

    zero = jnp.zeros_like(d)
    forward, adjoint, shifted = ([zero], [zero], [zero])
    for i in range(BLOCK):
        forward.append(d * forward[i] + source(0, i))
        shifted.append(source(2, i))
    for i in range(BLOCK - 1, -1, -1):
        adjoint.append(d * adjoint[-1] + source(1, i))
    adjoint = adjoint[::-1][1:]
    gradient = [source(3, i) for i in range(BLOCK)]
    while len(gradient) > 1:
        gradient = [a + b for a, b in zip(gradient[::2], gradient[1::2])]
    first = jnp.where(block == BLOCKS - 1, source(0, BLOCK - 1), forward[BLOCK])
    whole = d * adjoint[0] + source(1, 0)
    totals = (first, whole, shifted[BLOCK], gradient[0])
    for b in range(BLOCKS):
        for n, value in enumerate(totals):
            totals_ref[b, n] = value
    for y in range(BLOCK // 2):
        for n, values in enumerate((forward, adjoint, shifted)):
            local_ref[y, n] = jnp.where(even, values[2 * y], values[2 * y + 1])


def spread_kernel(totals_ref, local_ref, own_ref, out_ref):
    d = owned_damping(own_ref)
    block = lax.axis_index("tm_0") * 8 + lax.axis_index("tm_1")
    even = lax.axis_index("tm_3") == 0
    d2 = d * d
    d4 = d2 * d2
    d16 = (d4 * d4) * (d4 * d4)
    entry = totals_ref[BLOCKS - 1, 0]
    for b in range(BLOCKS - 1):
        entry = jnp.where(b < block, d16 * entry + totals_ref[b, 0], entry)
    after = jnp.zeros_like(d)
    for b in range(BLOCKS - 1, 0, -1):
        after = jnp.where(b > block, d16 * after + totals_ref[b, 1], after)
    before = totals_ref[(block + BLOCKS - 1) % BLOCKS, 2]
    gradient = [totals_ref[b, 3] for b in range(BLOCKS)]
    while len(gradient) > 1:
        gradient = [a + b for a, b in zip(gradient[::2], gradient[1::2])]
    gradient = gradient[0] * (1.0 / (COARSEN * SLABS))
    entry = jnp.where(even, entry, d * entry)
    after = jnp.where(even, d * after, after)
    half = BLOCK // 2
    for y in range(half):
        out_ref[y, 0] = local_ref[y, 0] + entry
        out_ref[y, 2] = gradient
        entry = d2 * entry
    for y in range(half - 1, -1, -1):
        shifted = local_ref[y, 2]
        if y == 0:
            shifted = jnp.where(even, before, shifted)
        out_ref[y, 1] = (local_ref[y, 1] + after) + shifted
        after = d2 * after


def finish_kernel(got_ref, keep_ref, order_ref, forward_ref, adjoint_ref, gradient_ref):
    def rows(n, h):
        return jnp.concatenate([got_ref[2 * t + h, n] for t in range(TILES)], 1)

    keep = jnp.concatenate([keep_ref[pl.ds(t * ROWS, ROWS), :] for t in range(TILES)], 1)
    forward, adjoint, gradient = (jnp.concatenate([rows(n, 0), rows(n, 1)], 0) for n in range(3))
    parts = jnp.concatenate([forward, adjoint + keep, gradient], 0)
    parts = reorder(parts, order_ref[...])
    forward_ref[...] = parts[0:ROWS]
    adjoint_ref[...] = parts[ROWS : 2 * ROWS]
    gradient_ref[...] = parts[2 * ROWS : 3 * ROWS]


def in_vmem(count):
    return [pl.BlockSpec(memory_space=pltpu.VMEM)] * count


def tiles(*lead):
    return pltpu.VMEM((*lead, 8, LANES), jnp.float32)


def in_place(value):
    return pltpu.with_memory_space_constraint(value, pltpu.VMEM)


def field_shape(*lead):
    return pltpu.VMEM((*lead, PHASES, TILES, 8, LANES), jnp.float32)


def relax_scratch():
    return [
        pltpu.VMEM((7, TILES, 2 * ROWS, LANES), jnp.float32),
        field_shape(7),
        field_shape(9),
        pltpu.VMEM((2, PHASES, TILES + 2 * SWEEPS, 8, LANES), jnp.float32),
        field_shape(COARSEN),
        field_shape(COARSEN - 1),
    ]


def shards(control, initial, diffusion, reaction, forward_guess, adjoint_guess, observed):
    own, order = pl.pallas_call(
        pack_kernel,
        out_shape=(pltpu.VMEM((7, ROWS, COLS), jnp.float32), pltpu.VMEM((COLS, COLS), jnp.bfloat16)),
        in_specs=[pl.BlockSpec(memory_space=pl.ANY)] * 7,
        out_specs=in_vmem(2),
        scratch_shapes=[
            pltpu.VMEM((7, ROWS, COLS), jnp.float32),
            pltpu.VMEM((COLS, COLS), jnp.bfloat16),
            pltpu.SemaphoreType.DMA((7,)),
        ],
        name="pack",
    )(control, initial, diffusion, reaction, forward_guess[0], adjoint_guess[0], observed[0])
    both = in_place(lax.all_gather(own, "space", axis=0))
    own = in_place(own)
    block = jax.ShapeDtypeStruct((ROWS, COLS), jnp.float32)
    channels, keep = pl.pallas_call(
        relax_kernel,
        out_shape=(tiles(8, 4), pltpu.VMEM((64, LANES), jnp.float32)),
        in_specs=in_vmem(2),
        out_specs=in_vmem(2),
        scratch_shapes=relax_scratch(),
        name="relax",
    )(own, both)
    got = lax.all_to_all(channels, "tm_2", 0, 0, tiled=True)
    got = in_place(lax.all_gather(got, "tm_3", axis=0))
    totals, local = pl.pallas_call(
        block_kernel,
        out_shape=(tiles(BLOCKS, 4), tiles(8, 3)),
        in_specs=in_vmem(2),
        out_specs=in_vmem(2),
        name="block",
    )(got, own)
    totals = in_place(lax.all_to_all(totals, ("tm_0", "tm_1"), 0, 0, tiled=True))
    sent = pl.pallas_call(
        spread_kernel, out_shape=tiles(8, 3), in_specs=in_vmem(3), out_specs=in_vmem(1)[0], name="spread"
    )(totals, in_place(local), own)
    back = in_place(lax.all_to_all(sent, "tm_2", 0, 0, tiled=True))
    keep, order = in_place(keep), in_place(order)
    forward_states, adjoint_states, gradient = pl.pallas_call(
        finish_kernel, out_shape=(block, block, block), in_specs=in_vmem(3), out_specs=in_vmem(3), name="finish"
    )(back, keep, order)
    return (forward_states[None], adjoint_states[None], gradient)


def solution(mesh):
    finer = Mesh(
        mesh.devices.reshape(2, 8, 8, 2, mesh.shape["space"]),
        ("tm_0", "tm_1", "tm_2", "tm_3", "space"),
    )
    return jax.shard_map(
        shards,
        mesh=finer,
        in_specs=(
            P("space", None),
            P("space", None),
            P("space", None),
            P("space", None),
            P(TM, "space", None),
            P(TM, "space", None),
            P(TM, "space", None),
        ),
        out_specs=(P(TM, "space", None), P(TM, "space", None), P("space", None)),
        check_vma=False,
    )
```

```python
import jax
import jax.numpy as jnp
from jax import lax
from jax.experimental import pallas as pl
from jax.experimental.pallas import tpu as pltpu
from jax.sharding import Mesh
from jax.sharding import PartitionSpec as P

SWEEPS = 3
COARSEN = 8
SLABS = 256
TM = ("tm_0", "tm_1", "tm_2", "tm_3")
ROWS = 16
COLS = 512
LANES = 128
TILES = COLS // LANES
PHASES = 4
BLOCK = 16
BLOCKS = SLABS // BLOCK

FORWARD, ADJOINT, TARGET, CONTROL, SPREAD, REACTION = range(6)
ARRAYS = 6
DAMPING, ALPHA, BETA, GAMMA, SOURCE, STATE, TOTAL, FW_LESS, AD_LESS, HEAD, HEAD_ADJOINT = range(11)


def tm_index():
    return ((lax.axis_index("tm_0") * 8 + lax.axis_index("tm_1")) * 8 + lax.axis_index("tm_2")) * 2 + lax.axis_index(
        "tm_3"
    )


def space_index():
    return lax.axis_index("space")


def each(fn, *fields):
    return [[fn(*cells) for cells in zip(*rows)] for rows in zip(*fields)]


def load(ref, *at):
    return [[ref[(*at, p, t)] for t in range(TILES)] for p in range(PHASES)]


def store(value, ref, *at):
    for p, row in enumerate(value):
        for t, cell in enumerate(row):
            ref[(*at, p, t)] = cell


def trim(field, count):
    return [row[count : len(row) - count] for row in field]


def make_stencil(space):
    sub = lax.broadcasted_iota(jnp.int32, (8, LANES), 0)
    lane = lax.broadcasted_iota(jnp.int32, (8, LANES), 1)
    up_ok = sub != 4 * space
    down_ok = sub != 7 - 4 * space
    first, last = (lane == 0, lane == LANES - 1)

    def widen(field, outside_zero):
        out = []
        for row in field:
            left = [pltpu.roll(cell, 1, 1) for cell in row[TILES - SWEEPS :]]
            right = [pltpu.roll(cell, LANES - 1, 1) for cell in row[:SWEEPS]]
            if outside_zero:
                left = [jnp.where(first, 0.0, cell) for cell in left]
                right = [jnp.where(last, 0.0, cell) for cell in right]
            out.append(left + row + right)
        return out

    def neighbours(field):
        above = [jnp.where(up_ok, pltpu.roll(cell, 1, 0), 0.0) for cell in field[-1][1:-1]]
        below = [jnp.where(down_ok, pltpu.roll(cell, 7, 0), 0.0) for cell in field[0][1:-1]]
        out = []
        pairs = [[u + a for u, a in zip(above, field[0][:-2])]]
        for p in range(1, PHASES):
            pairs.append([u + a for u, a in zip(field[p - 1][1:], field[p][:-1])])
        pairs.append([b + d for b, d in zip(field[-1][2:], below)])
        for p in range(PHASES):
            upper = pairs[p][:-1] if p else pairs[p]
            lower = pairs[p + 1][1:] if p < PHASES - 1 else pairs[p + 1]
            out.append([x + y for x, y in zip(upper, lower)])
        return out

    return widen, neighbours


def exact_terms(value):
    high = value.astype(jnp.bfloat16)
    rest = value - high.astype(jnp.float32)
    middle = rest.astype(jnp.bfloat16)
    low = (rest - middle.astype(jnp.float32)).astype(jnp.bfloat16)
    return high, middle, low


def reorder(value, selection):
    high, middle, low = (
        jnp.dot(term, selection, preferred_element_type=jnp.float32)
        for term in exact_terms(value)
    )
    return high + (middle + low)


def pack_kernel(control, initial, diffusion, reaction, forward, adjoint, observed, out_ref, order_ref, raw, into, sems):
    is_first = tm_index() == 0

    def copy(source, slot):
        return pltpu.make_async_copy(source, raw.at[slot], sems.at[slot])

    @pl.when(is_first)
    def _():
        copy(initial, ADJOINT).start()

    @pl.when(jnp.logical_not(is_first))
    def _():
        copy(adjoint, ADJOINT).start()

    rest = (
        (forward, FORWARD),
        (observed, TARGET),
        (control, CONTROL),
        (diffusion, SPREAD),
        (reaction, REACTION),
    )
    for source, slot in rest:
        copy(source, slot).start()
    column, lane = (lax.broadcasted_iota(jnp.int32, (LANES, COLS), d) for d in (1, 0))
    for t in range(TILES):
        order_ref[t * LANES : (t + 1) * LANES, :] = jnp.where(column == TILES * lane + t, 1.0, 0.0).astype(jnp.bfloat16)
    column, lane = (lax.broadcasted_iota(jnp.int32, (COLS, LANES), d) for d in (0, 1))
    for t in range(TILES):
        into[:, t * LANES : (t + 1) * LANES] = jnp.where(column == TILES * lane + t, 1.0, 0.0).astype(jnp.bfloat16)
    copy(adjoint, ADJOINT).wait()
    for source, slot in rest:
        copy(source, slot).wait()
    packed = reorder(raw[...].reshape(ARRAYS * ROWS, COLS), into[...])
    out_ref[...] = packed.reshape(ARRAYS, ROWS, COLS)


def relax_kernel(own_ref, both_ref, chan_ref, keep_ref, raw, grid, field, wide, points, coarse_points):
    slab = tm_index()
    space = space_index()
    widen, neighbours = make_stencil(space)
    not_last = jnp.where(slab == SLABS - 1, 0.0, 1.0)
    not_first = jnp.where(slab == 0, 0.0, 1.0)

    for n in range(ARRAYS):
        for t in range(TILES):
            cols = pl.ds(t * LANES, LANES)
            raw[n, t, 0:ROWS, :] = own_ref[n, :, cols]
            raw[n, t, ROWS : 2 * ROWS, :] = both_ref[1 - space, n, :, cols]
    for n in range(ARRAYS):
        for p in range(PHASES):
            for t in range(TILES):
                grid[n, p, t] = raw[n, t, pl.ds(p, 8, stride=PHASES), :]

    spread, reaction = (load(grid, SPREAD), load(grid, REACTION))
    inverse = each(lambda s, r: 1.0 / (1.0 + 4.0 * s + r), spread, reaction)
    store(widen(inverse, True), wide, 0)
    store(widen(each(jnp.multiply, spread, inverse), True), wide, 1)
    damping = each(lambda r: 1.0 / (1.0 + COARSEN * r), reaction)
    store(damping, field, DAMPING)

    def inverse_wide(count):
        return [[wide[0, p, t] for t in range(SWEEPS - count, SWEEPS + TILES + count)] for p in range(PHASES)]

    def weight_wide(count):
        return [[wide[1, p, t] for t in range(SWEEPS - count, SWEEPS + TILES + count)] for p in range(PHASES)]

    def forward_step(right_side):
        v = widen(right_side, True)
        scaled = each(jnp.multiply, inverse_wide(SWEEPS - 1), trim(v, 1))
        for n in range(SWEEPS):
            v = each(
                lambda s, w, q: s + w * q, trim(scaled, n), weight_wide(SWEEPS - 1 - n), neighbours(v)
            )
        return v

    def adjoint_step(y):
        carried, summed = (widen(y, False), y)
        for n in range(SWEEPS - 1):
            carried = neighbours(each(jnp.multiply, weight_wide(SWEEPS - n), carried))
            summed = each(jnp.add, summed, trim(carried, SWEEPS - 1 - n))
        final = neighbours(each(jnp.multiply, weight_wide(1), carried))
        return each(lambda s, i, f: s * i + f, summed, inverse_wide(0), final)

    store(load(grid, FORWARD), field, STATE)
    store(load(grid, ADJOINT), field, BETA)
    store(each(lambda g: g / COARSEN, load(grid, FORWARD)), field, GAMMA)

    def forward_body(i, _):
        v = forward_step(each(jnp.add, load(field, STATE), load(grid, CONTROL)))
        beta = adjoint_step(load(field, BETA))
        gamma = adjoint_step(each(lambda a, o: a - o / COARSEN, load(field, GAMMA), load(grid, TARGET)))
        store(v, field, STATE)
        store(v, points, i)
        store(beta, field, BETA)
        store(gamma, field, GAMMA)
        return 0

    lax.fori_loop(0, COARSEN, forward_body, 0)

    zeros = each(jnp.zeros_like, damping)
    store(zeros, field, HEAD)
    store(zeros, field, HEAD_ADJOINT)

    @pl.when(slab == 0)
    def _():
        store(load(grid, ADJOINT), field, HEAD)

        def head_body(i, _):
            v = forward_step(each(jnp.add, load(field, HEAD), load(grid, CONTROL)))
            store(v, field, HEAD)
            store(v, coarse_points, i)
            return 0

        def head_adjoint_body(n, _):
            at = COARSEN - 2 - n
            v = each(lambda a, f: a + f / COARSEN, load(field, HEAD_ADJOINT), load(coarse_points, at))
            store(adjoint_step(v), field, HEAD_ADJOINT)
            return 0

        lax.fori_loop(0, COARSEN, head_body, 0)
        lax.fori_loop(0, COARSEN - 1, head_adjoint_body, 0)

    forward_less = jnp.maximum(SLABS - 2 - slab, 0)
    adjoint_less = jnp.maximum(slab - 1, 0)
    for slot, count in ((FW_LESS, forward_less), (AD_LESS, adjoint_less)):
        power, block = (damping, each(jnp.ones_like, damping))
        total = each(jnp.zeros_like, damping)
        for b in range(8):
            taken = ((count >> b) & 1) == 1
            total = each(lambda s, v, q: jnp.where(taken, v + q * s, s), total, block, power)
            if b < 7:
                block = each(lambda v, q: v + v * q, block, power)
                power = each(lambda q: q * q, power)
        store(total, field, slot)

    head = load(field, HEAD)
    push = each(
        lambda f, d, g, h: f - d * (g - h), load(field, STATE), load(field, DAMPING), load(grid, FORWARD), head
    )
    store(push, field, SOURCE)
    store(
        each(
            lambda w, u, h, e: w * u + (h + (1.0 - not_first) * e),
            load(field, FW_LESS),
            push,
            head,
            load(grid, ADJOINT),
        ),
        field,
        STATE,
    )
    store(each(jnp.zeros_like, push), field, ALPHA)

    def adjoint_body(n, _):
        at = COARSEN - 2 - n
        alpha = adjoint_step(each(lambda a, f: a + f / COARSEN, load(field, ALPHA), load(points, at)))
        v = forward_step(each(jnp.add, load(field, STATE), load(grid, CONTROL)))
        store(alpha, field, ALPHA)
        store(v, field, STATE)
        store(v, coarse_points, n)
        return 0

    lax.fori_loop(0, COARSEN - 1, adjoint_body, 0, unroll=True)

    damping = load(field, DAMPING)
    alpha, beta, gamma = (load(field, ALPHA), load(field, BETA), load(field, GAMMA))
    keep = each(
        lambda g, d, a, h: g + not_last * (d * a) + h, gamma, damping, alpha, load(field, HEAD_ADJOINT)
    )
    pull = each(lambda k, d, g, b: d * (k - g) + b, keep, damping, load(grid, ADJOINT), beta)
    push = load(field, SOURCE)
    less = load(field, AD_LESS)
    store(
        each(lambda a, k, w, q, d: not_last * a + k + not_first * ((1.0 + d * w) * q), alpha, keep, less, pull, damping),
        field,
        TOTAL,
    )
    rest = each(lambda a, k, w, q: not_last * a + not_first * (k + w * q), alpha, keep, less, pull)
    store(
        each(
            lambda t, w, d, u, h, o: t + (not_last * ((1.0 + d * w) * u) + h - o) / COARSEN,
            rest,
            load(field, FW_LESS),
            damping,
            push,
            load(field, HEAD),
            load(grid, TARGET),
        ),
        field,
        GAMMA,
    )
    store(pull, field, BETA)
    store(keep, field, STATE)

    def gradient_body(n, _):
        v = adjoint_step(load(field, GAMMA))
        store(each(jnp.add, load(field, TOTAL), v), field, TOTAL)
        at = COARSEN - 2 - n
        store(
            each(lambda a, f, o: a + (f - o) / COARSEN, v, load(coarse_points, at), load(grid, TARGET)), field, GAMMA
        )
        return 0

    lax.fori_loop(0, COARSEN - 1, gradient_body, 0, unroll=True)

    for n, slot in enumerate((SOURCE, BETA, ALPHA, TOTAL)):
        for p in range(PHASES):
            for t in range(TILES):
                raw[n, t, pl.ds(p, 4, stride=PHASES), :] = field[slot, p, t, 0:4, :]
    for n in range(4):
        for t in range(TILES):
            for h in range(2):
                chan_ref[2 * t + h, n] = raw[n, t, 8 * h : 8 * h + 8, :]
    for n, slot in enumerate((HEAD, STATE)):
        for p in range(PHASES):
            for t in range(TILES):
                at = (n * TILES + t) * ROWS + p
                keep_ref[pl.ds(at, 4, stride=PHASES), :] = field[slot, p, t, 0:4, :]


def owned_damping(own_ref):
    owner = lax.axis_index("tm_2")
    rows = own_ref[REACTION, pl.ds(pl.multiple_of(8 * (owner % 2), 8), 8), :]
    reaction = rows[:, 0:LANES]
    for t in range(1, TILES):
        reaction = jnp.where(owner // 2 == t, rows[:, t * LANES : (t + 1) * LANES], reaction)
    return 1.0 / (1.0 + COARSEN * reaction)


def block_kernel(got_ref, own_ref, totals_ref, local_ref):
    d = owned_damping(own_ref)
    block = lax.axis_index("tm_0") * 8 + lax.axis_index("tm_1")
    even = lax.axis_index("tm_3") == 0

    def source(n, i):
        return got_ref[i % 2, i // 2, n]

    zero = jnp.zeros_like(d)
    forward, adjoint, shifted = ([zero], [zero], [zero])
    for i in range(BLOCK):
        forward.append(d * forward[i] + source(0, i))
        shifted.append(source(2, i))
    for i in range(BLOCK - 1, -1, -1):
        adjoint.append(d * adjoint[-1] + source(1, i))
    adjoint = adjoint[::-1][1:]
    gradient = [source(3, i) for i in range(BLOCK)]
    while len(gradient) > 1:
        gradient = [a + b for a, b in zip(gradient[::2], gradient[1::2])]
    whole = d * adjoint[0] + source(1, 0)
    for b in range(BLOCKS):
        totals_ref[b, 0] = jnp.where(b > block, forward[BLOCK], whole)
        totals_ref[b, 1] = shifted[BLOCK]
        totals_ref[b, 2] = gradient[0]
    for y in range(BLOCK // 2):
        for n, values in enumerate((forward, adjoint, shifted)):
            local_ref[y, n] = jnp.where(even, values[2 * y], values[2 * y + 1])


def spread_kernel(totals_ref, local_ref, own_ref, out_ref):
    d = owned_damping(own_ref)
    block = lax.axis_index("tm_0") * 8 + lax.axis_index("tm_1")
    even = lax.axis_index("tm_3") == 0
    d2 = d * d
    d4 = d2 * d2
    d16 = (d4 * d4) * (d4 * d4)
    entry = jnp.zeros_like(d)
    for b in range(BLOCKS - 1):
        entry = jnp.where(b < block, d16 * entry + totals_ref[b, 0], entry)
    after = jnp.zeros_like(d)
    for b in range(BLOCKS - 1, 0, -1):
        after = jnp.where(b > block, d16 * after + totals_ref[b, 0], after)
    before = jnp.where(block > 0, totals_ref[jnp.maximum(block - 1, 0), 1], 0.0)
    gradient = [totals_ref[b, 2] for b in range(BLOCKS)]
    while len(gradient) > 1:
        gradient = [a + b for a, b in zip(gradient[::2], gradient[1::2])]
    gradient = gradient[0] * (1.0 / (COARSEN * SLABS))
    entry = jnp.where(even, entry, d * entry)
    after = jnp.where(even, d * after, after)
    half = BLOCK // 2
    for y in range(half):
        out_ref[y, 0] = local_ref[y, 0] + entry
        out_ref[y, 2] = gradient
        entry = d2 * entry
    for y in range(half - 1, -1, -1):
        shifted = local_ref[y, 2]
        if y == 0:
            shifted = jnp.where(even, before, shifted)
        out_ref[y, 1] = (local_ref[y, 1] + after) + shifted
        after = d2 * after


def finish_kernel(got_ref, keep_ref, order_ref, forward_ref, adjoint_ref, gradient_ref):
    def rows(n, h):
        return jnp.concatenate([got_ref[2 * t + h, n] for t in range(TILES)], 1)

    head, keep = (
        jnp.concatenate([keep_ref[pl.ds((n * TILES + t) * ROWS, ROWS), :] for t in range(TILES)], 1) for n in range(2)
    )
    forward, adjoint, gradient = (jnp.concatenate([rows(n, 0), rows(n, 1)], 0) for n in range(3))
    parts = jnp.concatenate([forward + head, adjoint + keep, gradient], 0)
    parts = reorder(parts, order_ref[...])
    forward_ref[...] = parts[0:ROWS]
    adjoint_ref[...] = parts[ROWS : 2 * ROWS]
    gradient_ref[...] = parts[2 * ROWS : 3 * ROWS]


def in_vmem(count):
    return [pl.BlockSpec(memory_space=pltpu.VMEM)] * count


def tiles(*lead):
    return pltpu.VMEM((*lead, 8, LANES), jnp.float32)


def in_place(value):
    return pltpu.with_memory_space_constraint(value, pltpu.VMEM)


def field_shape(*lead):
    return pltpu.VMEM((*lead, PHASES, TILES, 8, LANES), jnp.float32)


def relax_scratch():
    return [
        pltpu.VMEM((ARRAYS, TILES, 2 * ROWS, LANES), jnp.float32),
        field_shape(ARRAYS),
        field_shape(11),
        pltpu.VMEM((2, PHASES, TILES + 2 * SWEEPS, 8, LANES), jnp.float32),
        field_shape(COARSEN),
        field_shape(COARSEN),
    ]


def shards(control, initial, diffusion, reaction, forward_guess, adjoint_guess, observed):
    own, order = pl.pallas_call(
        pack_kernel,
        out_shape=(pltpu.VMEM((ARRAYS, ROWS, COLS), jnp.float32), pltpu.VMEM((COLS, COLS), jnp.bfloat16)),
        in_specs=[pl.BlockSpec(memory_space=pl.ANY)] * 7,
        out_specs=in_vmem(2),
        scratch_shapes=[
            pltpu.VMEM((ARRAYS, ROWS, COLS), jnp.float32),
            pltpu.VMEM((COLS, COLS), jnp.bfloat16),
            pltpu.SemaphoreType.DMA((ARRAYS,)),
        ],
        name="pack",
    )(control, initial, diffusion, reaction, forward_guess[0], adjoint_guess[0], observed[0])
    both = in_place(lax.all_gather(own, "space", axis=0))
    own = in_place(own)
    block = jax.ShapeDtypeStruct((ROWS, COLS), jnp.float32)
    channels, keep = pl.pallas_call(
        relax_kernel,
        out_shape=(tiles(8, 4), pltpu.VMEM((128, LANES), jnp.float32)),
        in_specs=in_vmem(2),
        out_specs=in_vmem(2),
        scratch_shapes=relax_scratch(),
        name="relax",
    )(own, both)
    got = lax.all_to_all(channels, "tm_2", 0, 0, tiled=True)
    got = in_place(lax.all_gather(got, "tm_3", axis=0))
    totals, local = pl.pallas_call(
        block_kernel,
        out_shape=(tiles(BLOCKS, 3), tiles(8, 3)),
        in_specs=in_vmem(2),
        out_specs=in_vmem(2),
        name="block",
    )(got, own)
    totals = in_place(lax.all_to_all(totals, ("tm_0", "tm_1"), 0, 0, tiled=True))
    sent = pl.pallas_call(
        spread_kernel, out_shape=tiles(8, 3), in_specs=in_vmem(3), out_specs=in_vmem(1)[0], name="spread"
    )(totals, in_place(local), own)
    back = in_place(lax.all_to_all(sent, "tm_2", 0, 0, tiled=True))
    keep, order = in_place(keep), in_place(order)
    forward_states, adjoint_states, gradient = pl.pallas_call(
        finish_kernel, out_shape=(block, block, block), in_specs=in_vmem(3), out_specs=in_vmem(3), name="finish"
    )(back, keep, order)
    return (forward_states[None], adjoint_states[None], gradient)


def solution(mesh):
    finer = Mesh(
        mesh.devices.reshape(2, 8, 8, 2, mesh.shape["space"]),
        ("tm_0", "tm_1", "tm_2", "tm_3", "space"),
    )
    return jax.shard_map(
        shards,
        mesh=finer,
        in_specs=(
            P("space", None),
            P("space", None),
            P("space", None),
            P("space", None),
            P(TM, "space", None),
            P(TM, "space", None),
            P(TM, "space", None),
        ),
        out_specs=(P(TM, "space", None), P(TM, "space", None), P("space", None)),
        check_vma=False,
    )
```

```python
import jax
import jax.numpy as jnp
from jax import lax
from jax.experimental import pallas as pl
from jax.experimental.pallas import tpu as pltpu
from jax.sharding import Mesh
from jax.sharding import PartitionSpec as P

SWEEPS = 3
COARSEN = 8
SLABS = 256
TM = ("tm_0", "tm_1", "tm_2", "tm_3")
ROWS = 16
COLS = 512
LANES = 128
TILES = COLS // LANES
PHASES = 4
BLOCK = 16
BLOCKS = SLABS // BLOCK

FORWARD, ADJOINT, TARGET, CONTROL, SPREAD, REACTION = range(6)
ARRAYS = 6
DAMPING, ALPHA, BETA, GAMMA, SOURCE, STATE, TOTAL, FW_LESS, AD_LESS, HEAD, HEAD_ADJOINT = range(11)


def tm_index():
    return ((lax.axis_index("tm_0") * 8 + lax.axis_index("tm_1")) * 8 + lax.axis_index("tm_2")) * 2 + lax.axis_index(
        "tm_3"
    )


def space_index():
    return lax.axis_index("space")


def each(fn, *fields):
    return [[fn(*cells) for cells in zip(*rows)] for rows in zip(*fields)]


def load(ref, *at):
    return [[ref[(*at, p, t)] for t in range(TILES)] for p in range(PHASES)]


def store(value, ref, *at):
    for p, row in enumerate(value):
        for t, cell in enumerate(row):
            ref[(*at, p, t)] = cell


def trim(field, count):
    return [row[count : len(row) - count] for row in field]


def make_stencil(space):
    sub = lax.broadcasted_iota(jnp.int32, (8, LANES), 0)
    lane = lax.broadcasted_iota(jnp.int32, (8, LANES), 1)
    up_ok = sub != 4 * space
    down_ok = sub != 7 - 4 * space
    first, last = (lane == 0, lane == LANES - 1)

    def widen(field, outside_zero):
        out = []
        for row in field:
            left = [pltpu.roll(cell, 1, 1) for cell in row[TILES - SWEEPS :]]
            right = [pltpu.roll(cell, LANES - 1, 1) for cell in row[:SWEEPS]]
            if outside_zero:
                left = [jnp.where(first, 0.0, cell) for cell in left]
                right = [jnp.where(last, 0.0, cell) for cell in right]
            out.append(left + row + right)
        return out

    def neighbours(field):
        above = [jnp.where(up_ok, pltpu.roll(cell, 1, 0), 0.0) for cell in field[-1][1:-1]]
        below = [jnp.where(down_ok, pltpu.roll(cell, 7, 0), 0.0) for cell in field[0][1:-1]]
        out = []
        pairs = [[u + a for u, a in zip(above, field[0][:-2])]]
        for p in range(1, PHASES):
            pairs.append([u + a for u, a in zip(field[p - 1][1:], field[p][:-1])])
        pairs.append([b + d for b, d in zip(field[-1][2:], below)])
        for p in range(PHASES):
            upper = pairs[p][:-1] if p else pairs[p]
            lower = pairs[p + 1][1:] if p < PHASES - 1 else pairs[p + 1]
            out.append([x + y for x, y in zip(upper, lower)])
        return out

    return widen, neighbours


def exact_terms(value):
    high = value.astype(jnp.bfloat16)
    rest = value - high.astype(jnp.float32)
    middle = rest.astype(jnp.bfloat16)
    low = (rest - middle.astype(jnp.float32)).astype(jnp.bfloat16)
    return high, middle, low


def reorder(value, selection):
    high, middle, low = (
        jnp.dot(term, selection, preferred_element_type=jnp.float32)
        for term in exact_terms(value)
    )
    return high + (middle + low)


def pack_kernel(control, initial, diffusion, reaction, forward, adjoint, observed, out_ref, order_ref, raw, into, sems):
    is_first = tm_index() == 0

    def copy(source, slot):
        return pltpu.make_async_copy(source, raw.at[slot], sems.at[slot])

    @pl.when(is_first)
    def _():
        copy(initial, ADJOINT).start()

    @pl.when(jnp.logical_not(is_first))
    def _():
        copy(adjoint, ADJOINT).start()

    rest = (
        (forward, FORWARD),
        (observed, TARGET),
        (control, CONTROL),
        (diffusion, SPREAD),
        (reaction, REACTION),
    )
    for source, slot in rest:
        copy(source, slot).start()
    column, lane = (lax.broadcasted_iota(jnp.int32, (LANES, COLS), d) for d in (1, 0))
    for t in range(TILES):
        order_ref[t * LANES : (t + 1) * LANES, :] = jnp.where(column == TILES * lane + t, 1.0, 0.0).astype(jnp.bfloat16)
    column, lane = (lax.broadcasted_iota(jnp.int32, (COLS, LANES), d) for d in (0, 1))
    for t in range(TILES):
        into[:, t * LANES : (t + 1) * LANES] = jnp.where(column == TILES * lane + t, 1.0, 0.0).astype(jnp.bfloat16)
    copy(adjoint, ADJOINT).wait()
    for source, slot in rest:
        copy(source, slot).wait()
    packed = reorder(raw[...].reshape(ARRAYS * ROWS, COLS), into[...])
    out_ref[...] = packed.reshape(ARRAYS, ROWS, COLS)


def relax_kernel(own_ref, both_ref, chan_ref, keep_ref, raw, grid, field, wide, points, coarse_points):
    slab = tm_index()
    space = space_index()
    widen, neighbours = make_stencil(space)
    not_last = jnp.where(slab == SLABS - 1, 0.0, 1.0)
    not_first = jnp.where(slab == 0, 0.0, 1.0)

    for n in range(ARRAYS):
        for t in range(TILES):
            cols = pl.ds(t * LANES, LANES)
            raw[n, t, 0:ROWS, :] = own_ref[n, :, cols]
            raw[n, t, ROWS : 2 * ROWS, :] = both_ref[1 - space, n, :, cols]
    for n in range(ARRAYS):
        for p in range(PHASES):
            for t in range(TILES):
                grid[n, p, t] = raw[n, t, pl.ds(p, 8, stride=PHASES), :]

    spread, reaction = (load(grid, SPREAD), load(grid, REACTION))
    inverse = each(lambda s, r: 1.0 / (1.0 + 4.0 * s + r), spread, reaction)
    store(widen(inverse, True), wide, 0)
    store(widen(each(jnp.multiply, spread, inverse), True), wide, 1)
    damping = each(lambda r: 1.0 / (1.0 + COARSEN * r), reaction)
    store(damping, field, DAMPING)

    def inverse_wide(count):
        return [[wide[0, p, t] for t in range(SWEEPS - count, SWEEPS + TILES + count)] for p in range(PHASES)]

    def weight_wide(count):
        return [[wide[1, p, t] for t in range(SWEEPS - count, SWEEPS + TILES + count)] for p in range(PHASES)]

    def forward_step(right_side):
        v = widen(right_side, True)
        scaled = each(jnp.multiply, inverse_wide(SWEEPS - 1), trim(v, 1))
        for n in range(SWEEPS):
            v = each(
                lambda s, w, q: s + w * q, trim(scaled, n), weight_wide(SWEEPS - 1 - n), neighbours(v)
            )
        return v

    def adjoint_step(y):
        carried, summed = (widen(y, False), y)
        for n in range(SWEEPS - 1):
            carried = neighbours(each(jnp.multiply, weight_wide(SWEEPS - n), carried))
            summed = each(jnp.add, summed, trim(carried, SWEEPS - 1 - n))
        final = neighbours(each(jnp.multiply, weight_wide(1), carried))
        return each(lambda s, i, f: s * i + f, summed, inverse_wide(0), final)

    v, beta = (load(grid, FORWARD), load(grid, ADJOINT))
    gamma = each(lambda g: g / COARSEN, load(grid, FORWARD))
    for i in range(COARSEN):
        v = forward_step(each(jnp.add, v, load(grid, CONTROL)))
        store(v, points, i)
        beta = adjoint_step(beta)
        gamma = adjoint_step(each(lambda a, o: a - o / COARSEN, gamma, load(grid, TARGET)))
    store(v, field, STATE)
    store(beta, field, BETA)
    store(gamma, field, GAMMA)

    zeros = each(jnp.zeros_like, damping)
    store(zeros, field, HEAD)
    store(zeros, field, HEAD_ADJOINT)

    @pl.when(slab == 0)
    def _():
        store(load(grid, ADJOINT), field, HEAD)

        def head_body(i, _):
            v = forward_step(each(jnp.add, load(field, HEAD), load(grid, CONTROL)))
            store(v, field, HEAD)
            store(v, coarse_points, i)
            return 0

        def head_adjoint_body(n, _):
            at = COARSEN - 2 - n
            v = each(lambda a, f: a + f / COARSEN, load(field, HEAD_ADJOINT), load(coarse_points, at))
            store(adjoint_step(v), field, HEAD_ADJOINT)
            return 0

        lax.fori_loop(0, COARSEN, head_body, 0)
        lax.fori_loop(0, COARSEN - 1, head_adjoint_body, 0)

    forward_less = jnp.maximum(SLABS - 2 - slab, 0)
    adjoint_less = jnp.maximum(slab - 1, 0)
    for slot, count in ((FW_LESS, forward_less), (AD_LESS, adjoint_less)):
        power, block = (damping, each(jnp.ones_like, damping))
        total = each(jnp.zeros_like, damping)
        for b in range(8):
            taken = ((count >> b) & 1) == 1
            total = each(lambda s, v, q: jnp.where(taken, v + q * s, s), total, block, power)
            if b < 7:
                block = each(lambda v, q: v + v * q, block, power)
                power = each(lambda q: q * q, power)
        store(total, field, slot)

    head = load(field, HEAD)
    push = each(
        lambda f, d, g, h: f - d * (g - h), load(field, STATE), load(field, DAMPING), load(grid, FORWARD), head
    )
    store(push, field, SOURCE)
    store(
        each(
            lambda w, u, h, e: w * u + (h + (1.0 - not_first) * e),
            load(field, FW_LESS),
            push,
            head,
            load(grid, ADJOINT),
        ),
        field,
        STATE,
    )
    v, alpha = (load(field, STATE), None)
    for n in range(COARSEN - 1):
        at = COARSEN - 2 - n
        misfit = each(lambda f: f / COARSEN, load(points, at))
        alpha = adjoint_step(misfit if alpha is None else each(jnp.add, alpha, misfit))
        v = forward_step(each(jnp.add, v, load(grid, CONTROL)))
        store(v, coarse_points, n)
    store(alpha, field, ALPHA)

    damping = load(field, DAMPING)
    alpha, beta, gamma = (load(field, ALPHA), load(field, BETA), load(field, GAMMA))
    keep = each(
        lambda g, d, a, h: g + not_last * (d * a) + h, gamma, damping, alpha, load(field, HEAD_ADJOINT)
    )
    pull = each(lambda k, d, g, b: d * (k - g) + b, keep, damping, load(grid, ADJOINT), beta)
    push = load(field, SOURCE)
    less = load(field, AD_LESS)
    store(
        each(lambda a, k, w, q, d: not_last * a + k + not_first * ((1.0 + d * w) * q), alpha, keep, less, pull, damping),
        field,
        TOTAL,
    )
    rest = each(lambda a, k, w, q: not_last * a + not_first * (k + w * q), alpha, keep, less, pull)
    store(
        each(
            lambda t, w, d, u, h, o: t + (not_last * ((1.0 + d * w) * u) + h - o) / COARSEN,
            rest,
            load(field, FW_LESS),
            damping,
            push,
            load(field, HEAD),
            load(grid, TARGET),
        ),
        field,
        GAMMA,
    )
    store(pull, field, BETA)
    store(keep, field, STATE)

    v, total = (load(field, GAMMA), load(field, TOTAL))
    for n in range(COARSEN - 1):
        v = adjoint_step(v)
        total = each(jnp.add, total, v)
        if n < COARSEN - 2:
            at = COARSEN - 2 - n
            v = each(lambda a, f, o: a + (f - o) / COARSEN, v, load(coarse_points, at), load(grid, TARGET))
    store(total, field, TOTAL)

    for n, slot in enumerate((SOURCE, BETA, ALPHA, TOTAL)):
        for p in range(PHASES):
            for t in range(TILES):
                raw[n, t, pl.ds(p, 4, stride=PHASES), :] = field[slot, p, t, 0:4, :]
    for n in range(4):
        for t in range(TILES):
            for h in range(2):
                chan_ref[2 * t + h, n] = raw[n, t, 8 * h : 8 * h + 8, :]
    for n, slot in enumerate((HEAD, STATE)):
        for p in range(PHASES):
            for t in range(TILES):
                at = (n * TILES + t) * ROWS + p
                keep_ref[pl.ds(at, 4, stride=PHASES), :] = field[slot, p, t, 0:4, :]


def owned_damping(own_ref):
    owner = lax.axis_index("tm_2")
    rows = own_ref[REACTION, pl.ds(pl.multiple_of(8 * (owner % 2), 8), 8), :]
    reaction = rows[:, 0:LANES]
    for t in range(1, TILES):
        reaction = jnp.where(owner // 2 == t, rows[:, t * LANES : (t + 1) * LANES], reaction)
    return 1.0 / (1.0 + COARSEN * reaction)


def block_kernel(got_ref, own_ref, totals_ref, local_ref):
    d = owned_damping(own_ref)
    block = lax.axis_index("tm_0") * 8 + lax.axis_index("tm_1")
    even = lax.axis_index("tm_3") == 0

    def source(n, i):
        return got_ref[i % 2, i // 2, n]

    zero = jnp.zeros_like(d)
    forward, adjoint, shifted = ([zero], [zero], [zero])
    for i in range(BLOCK):
        forward.append(d * forward[i] + source(0, i))
        shifted.append(source(2, i))
    for i in range(BLOCK - 1, -1, -1):
        adjoint.append(d * adjoint[-1] + source(1, i))
    adjoint = adjoint[::-1][1:]
    gradient = [source(3, i) for i in range(BLOCK)]
    while len(gradient) > 1:
        gradient = [a + b for a, b in zip(gradient[::2], gradient[1::2])]
    whole = d * adjoint[0] + source(1, 0)
    for b in range(BLOCKS):
        totals_ref[b, 0] = jnp.where(b > block, forward[BLOCK], whole)
        totals_ref[b, 1] = shifted[BLOCK]
        totals_ref[b, 2] = gradient[0]
    for y in range(BLOCK // 2):
        for n, values in enumerate((forward, adjoint, shifted)):
            local_ref[y, n] = jnp.where(even, values[2 * y], values[2 * y + 1])


def spread_kernel(totals_ref, local_ref, own_ref, out_ref):
    d = owned_damping(own_ref)
    block = lax.axis_index("tm_0") * 8 + lax.axis_index("tm_1")
    even = lax.axis_index("tm_3") == 0
    d2 = d * d
    d4 = d2 * d2
    d16 = (d4 * d4) * (d4 * d4)
    entry = jnp.zeros_like(d)
    for b in range(BLOCKS - 1):
        entry = jnp.where(b < block, d16 * entry + totals_ref[b, 0], entry)
    after = jnp.zeros_like(d)
    for b in range(BLOCKS - 1, 0, -1):
        after = jnp.where(b > block, d16 * after + totals_ref[b, 0], after)
    before = jnp.where(block > 0, totals_ref[jnp.maximum(block - 1, 0), 1], 0.0)
    gradient = [totals_ref[b, 2] for b in range(BLOCKS)]
    while len(gradient) > 1:
        gradient = [a + b for a, b in zip(gradient[::2], gradient[1::2])]
    gradient = gradient[0] * (1.0 / (COARSEN * SLABS))
    entry = jnp.where(even, entry, d * entry)
    after = jnp.where(even, d * after, after)
    half = BLOCK // 2
    for y in range(half):
        out_ref[y, 0] = local_ref[y, 0] + entry
        out_ref[y, 2] = gradient
        entry = d2 * entry
    for y in range(half - 1, -1, -1):
        shifted = local_ref[y, 2]
        if y == 0:
            shifted = jnp.where(even, before, shifted)
        out_ref[y, 1] = (local_ref[y, 1] + after) + shifted
        after = d2 * after


def finish_kernel(got_ref, keep_ref, order_ref, forward_ref, adjoint_ref, gradient_ref):
    def rows(n, h):
        return jnp.concatenate([got_ref[2 * t + h, n] for t in range(TILES)], 1)

    head, keep = (
        jnp.concatenate([keep_ref[pl.ds((n * TILES + t) * ROWS, ROWS), :] for t in range(TILES)], 1) for n in range(2)
    )
    forward, adjoint, gradient = (jnp.concatenate([rows(n, 0), rows(n, 1)], 0) for n in range(3))
    parts = jnp.concatenate([forward + head, adjoint + keep, gradient], 0)
    parts = reorder(parts, order_ref[...])
    forward_ref[...] = parts[0:ROWS]
    adjoint_ref[...] = parts[ROWS : 2 * ROWS]
    gradient_ref[...] = parts[2 * ROWS : 3 * ROWS]


def in_vmem(count):
    return [pl.BlockSpec(memory_space=pltpu.VMEM)] * count


def tiles(*lead):
    return pltpu.VMEM((*lead, 8, LANES), jnp.float32)


def in_place(value):
    return pltpu.with_memory_space_constraint(value, pltpu.VMEM)


def field_shape(*lead):
    return pltpu.VMEM((*lead, PHASES, TILES, 8, LANES), jnp.float32)


def relax_scratch():
    return [
        pltpu.VMEM((ARRAYS, TILES, 2 * ROWS, LANES), jnp.float32),
        field_shape(ARRAYS),
        field_shape(11),
        pltpu.VMEM((2, PHASES, TILES + 2 * SWEEPS, 8, LANES), jnp.float32),
        field_shape(COARSEN),
        field_shape(COARSEN),
    ]


def shards(control, initial, diffusion, reaction, forward_guess, adjoint_guess, observed):
    own, order = pl.pallas_call(
        pack_kernel,
        out_shape=(pltpu.VMEM((ARRAYS, ROWS, COLS), jnp.float32), pltpu.VMEM((COLS, COLS), jnp.bfloat16)),
        in_specs=[pl.BlockSpec(memory_space=pl.ANY)] * 7,
        out_specs=in_vmem(2),
        scratch_shapes=[
            pltpu.VMEM((ARRAYS, ROWS, COLS), jnp.float32),
            pltpu.VMEM((COLS, COLS), jnp.bfloat16),
            pltpu.SemaphoreType.DMA((ARRAYS,)),
        ],
        name="pack",
    )(control, initial, diffusion, reaction, forward_guess[0], adjoint_guess[0], observed[0])
    both = in_place(lax.all_gather(own, "space", axis=0))
    own = in_place(own)
    block = jax.ShapeDtypeStruct((ROWS, COLS), jnp.float32)
    channels, keep = pl.pallas_call(
        relax_kernel,
        out_shape=(tiles(8, 4), pltpu.VMEM((128, LANES), jnp.float32)),
        in_specs=in_vmem(2),
        out_specs=in_vmem(2),
        scratch_shapes=relax_scratch(),
        name="relax",
    )(own, both)
    got = lax.all_to_all(channels, "tm_2", 0, 0, tiled=True)
    got = in_place(lax.all_gather(got, "tm_3", axis=0))
    totals, local = pl.pallas_call(
        block_kernel,
        out_shape=(tiles(BLOCKS, 3), tiles(8, 3)),
        in_specs=in_vmem(2),
        out_specs=in_vmem(2),
        name="block",
    )(got, own)
    totals = in_place(lax.all_to_all(totals, ("tm_0", "tm_1"), 0, 0, tiled=True))
    sent = pl.pallas_call(
        spread_kernel, out_shape=tiles(8, 3), in_specs=in_vmem(3), out_specs=in_vmem(1)[0], name="spread"
    )(totals, in_place(local), own)
    back = in_place(lax.all_to_all(sent, "tm_2", 0, 0, tiled=True))
    keep, order = in_place(keep), in_place(order)
    forward_states, adjoint_states, gradient = pl.pallas_call(
        finish_kernel, out_shape=(block, block, block), in_specs=in_vmem(3), out_specs=in_vmem(3), name="finish"
    )(back, keep, order)
    return (forward_states[None], adjoint_states[None], gradient)


def solution(mesh):
    finer = Mesh(
        mesh.devices.reshape(2, 8, 8, 2, mesh.shape["space"]),
        ("tm_0", "tm_1", "tm_2", "tm_3", "space"),
    )
    return jax.shard_map(
        shards,
        mesh=finer,
        in_specs=(
            P("space", None),
            P("space", None),
            P("space", None),
            P("space", None),
            P(TM, "space", None),
            P(TM, "space", None),
            P(TM, "space", None),
        ),
        out_specs=(P(TM, "space", None), P(TM, "space", None), P("space", None)),
        check_vma=False,
    )
```

```python
import jax
import jax.numpy as jnp
from jax import lax
from jax.experimental import pallas as pl
from jax.experimental.pallas import tpu as pltpu
from jax.sharding import Mesh
from jax.sharding import PartitionSpec as P

SWEEPS = 3
COARSEN = 8
SLABS = 256
TM = ("tm_0", "tm_1", "tm_2", "tm_3")
ROWS = 16
COLS = 512
LANES = 128
TILES = COLS // LANES
PHASES = 4
BLOCK = 16
BLOCKS = SLABS // BLOCK

FORWARD, ADJOINT, TARGET, CONTROL, SPREAD, REACTION = range(6)
ARRAYS = 6
DAMPING, ALPHA, BETA, GAMMA, SOURCE, STATE, TOTAL, FW_LESS, AD_LESS, HEAD, HEAD_ADJOINT = range(11)


def tm_index():
    return ((lax.axis_index("tm_0") * 8 + lax.axis_index("tm_1")) * 8 + lax.axis_index("tm_2")) * 2 + lax.axis_index(
        "tm_3"
    )


def space_index():
    return lax.axis_index("space")


def each(fn, *fields):
    return [[fn(*cells) for cells in zip(*rows)] for rows in zip(*fields)]


def load(ref, *at):
    return [[ref[(*at, p, t)] for t in range(TILES)] for p in range(PHASES)]


def store(value, ref, *at):
    for p, row in enumerate(value):
        for t, cell in enumerate(row):
            ref[(*at, p, t)] = cell


def trim(field, count):
    return [row[count : len(row) - count] for row in field]


def inside():
    lane = lax.broadcasted_iota(jnp.int32, (8, LANES), 1)
    left, right = (jnp.where(lane == edge, 0.0, 1.0) for edge in (0, LANES - 1))
    return [[left] * SWEEPS + [jnp.ones_like(left)] * TILES + [right] * SWEEPS] * PHASES


def make_stencil(space):
    sub = lax.broadcasted_iota(jnp.int32, (8, LANES), 0)
    lane = lax.broadcasted_iota(jnp.int32, (8, LANES), 1)
    up_ok = sub != 4 * space
    down_ok = sub != 7 - 4 * space
    first, last = (lane == 0, lane == LANES - 1)

    def widen(field):
        out = []
        for row in field:
            left = [pltpu.roll(cell, 1, 1) for cell in row[TILES - SWEEPS :]]
            right = [pltpu.roll(cell, LANES - 1, 1) for cell in row[:SWEEPS]]
            left[-1] = jnp.where(first, 0.0, left[-1])
            right[0] = jnp.where(last, 0.0, right[0])
            out.append(left + row + right)
        return out

    def neighbours(field):
        above = [jnp.where(up_ok, pltpu.roll(cell, 1, 0), 0.0) for cell in field[-1][1:-1]]
        below = [jnp.where(down_ok, pltpu.roll(cell, 7, 0), 0.0) for cell in field[0][1:-1]]
        out = []
        pairs = [[u + a for u, a in zip(above, field[0][:-2])]]
        for p in range(1, PHASES):
            pairs.append([u + a for u, a in zip(field[p - 1][1:], field[p][:-1])])
        pairs.append([b + d for b, d in zip(field[-1][2:], below)])
        for p in range(PHASES):
            upper = pairs[p][:-1] if p else pairs[p]
            lower = pairs[p + 1][1:] if p < PHASES - 1 else pairs[p + 1]
            out.append([x + y for x, y in zip(upper, lower)])
        return out

    return widen, neighbours


def exact_terms(value):
    high = value.astype(jnp.bfloat16)
    rest = value - high.astype(jnp.float32)
    middle = rest.astype(jnp.bfloat16)
    low = (rest - middle.astype(jnp.float32)).astype(jnp.bfloat16)
    return high, middle, low


def reorder(value, selection):
    high, middle, low = (
        jnp.dot(term, selection, preferred_element_type=jnp.float32)
        for term in exact_terms(value)
    )
    return high + (middle + low)


def pack_kernel(control, initial, diffusion, reaction, forward, adjoint, observed, out_ref, order_ref, raw, into, sems):
    is_first = tm_index() == 0

    def copy(source, slot):
        return pltpu.make_async_copy(source, raw.at[slot], sems.at[slot])

    @pl.when(is_first)
    def _():
        copy(initial, ADJOINT).start()

    @pl.when(jnp.logical_not(is_first))
    def _():
        copy(adjoint, ADJOINT).start()

    rest = (
        (forward, FORWARD),
        (observed, TARGET),
        (control, CONTROL),
        (diffusion, SPREAD),
        (reaction, REACTION),
    )
    for source, slot in rest:
        copy(source, slot).start()
    column, lane = (lax.broadcasted_iota(jnp.int32, (LANES, COLS), d) for d in (1, 0))
    for t in range(TILES):
        order_ref[t * LANES : (t + 1) * LANES, :] = jnp.where(column == TILES * lane + t, 1.0, 0.0).astype(jnp.bfloat16)
    column, lane = (lax.broadcasted_iota(jnp.int32, (COLS, LANES), d) for d in (0, 1))
    for t in range(TILES):
        into[:, t * LANES : (t + 1) * LANES] = jnp.where(column == TILES * lane + t, 1.0, 0.0).astype(jnp.bfloat16)
    copy(adjoint, ADJOINT).wait()
    for source, slot in rest:
        copy(source, slot).wait()
    packed = reorder(raw[...].reshape(ARRAYS * ROWS, COLS), into[...])
    out_ref[...] = packed.reshape(ARRAYS, ROWS, COLS)


def relax_kernel(own_ref, both_ref, chan_ref, keep_ref, raw, grid, field, wide, points, coarse_points):
    slab = tm_index()
    space = space_index()
    widen, neighbours = make_stencil(space)
    not_last = jnp.where(slab == SLABS - 1, 0.0, 1.0)
    not_first = jnp.where(slab == 0, 0.0, 1.0)

    for n in range(ARRAYS):
        for t in range(TILES):
            cols = pl.ds(t * LANES, LANES)
            raw[n, t, 0:ROWS, :] = own_ref[n, :, cols]
            raw[n, t, ROWS : 2 * ROWS, :] = both_ref[1 - space, n, :, cols]
    for n in range(ARRAYS):
        for p in range(PHASES):
            for t in range(TILES):
                grid[n, p, t] = raw[n, t, pl.ds(p, 8, stride=PHASES), :]

    spread, reaction = (load(grid, SPREAD), load(grid, REACTION))
    inverse = each(lambda s, r: 1.0 / (1.0 + 4.0 * s + r), spread, reaction)
    store(each(jnp.multiply, inside(), widen(inverse)), wide, 0)
    store(each(jnp.multiply, inside(), widen(each(jnp.multiply, spread, inverse))), wide, 1)
    damping = each(lambda r: 1.0 / (1.0 + COARSEN * r), reaction)
    store(damping, field, DAMPING)

    def inverse_wide(count):
        return [[wide[0, p, t] for t in range(SWEEPS - count, SWEEPS + TILES + count)] for p in range(PHASES)]

    def weight_wide(count):
        return [[wide[1, p, t] for t in range(SWEEPS - count, SWEEPS + TILES + count)] for p in range(PHASES)]

    def forward_step(right_side):
        v = widen(right_side)
        scaled = each(jnp.multiply, inverse_wide(SWEEPS - 1), trim(v, 1))
        for n in range(SWEEPS):
            v = each(
                lambda s, w, q: s + w * q, trim(scaled, n), weight_wide(SWEEPS - 1 - n), neighbours(v)
            )
        return v

    def adjoint_step(y):
        carried, summed = (widen(each(jnp.multiply, weight_wide(0), y)), y)
        for n in range(SWEEPS - 1):
            carried = neighbours(carried)
            summed = each(jnp.add, summed, trim(carried, SWEEPS - 1 - n))
            carried = each(jnp.multiply, weight_wide(SWEEPS - 1 - n), carried)
        final = neighbours(carried)
        return each(lambda s, i, f: s * i + f, summed, inverse_wide(0), final)

    v, beta = (load(grid, FORWARD), load(grid, ADJOINT))
    gamma = each(lambda g: g / COARSEN, load(grid, FORWARD))
    for i in range(COARSEN):
        v = forward_step(each(jnp.add, v, load(grid, CONTROL)))
        store(v, points, i)
        beta = adjoint_step(beta)
        gamma = adjoint_step(each(lambda a, o: a - o / COARSEN, gamma, load(grid, TARGET)))
    store(v, field, STATE)
    store(beta, field, BETA)
    store(gamma, field, GAMMA)

    zeros = each(jnp.zeros_like, damping)
    store(zeros, field, HEAD)
    store(zeros, field, HEAD_ADJOINT)

    @pl.when(slab == 0)
    def _():
        store(load(grid, ADJOINT), field, HEAD)

        def head_body(i, _):
            v = forward_step(each(jnp.add, load(field, HEAD), load(grid, CONTROL)))
            store(v, field, HEAD)
            store(v, coarse_points, i)
            return 0

        def head_adjoint_body(n, _):
            at = COARSEN - 2 - n
            v = each(lambda a, f: a + f / COARSEN, load(field, HEAD_ADJOINT), load(coarse_points, at))
            store(adjoint_step(v), field, HEAD_ADJOINT)
            return 0

        lax.fori_loop(0, COARSEN, head_body, 0)
        lax.fori_loop(0, COARSEN - 1, head_adjoint_body, 0)

    forward_less = jnp.maximum(SLABS - 2 - slab, 0)
    adjoint_less = jnp.maximum(slab - 1, 0)
    for slot, count in ((FW_LESS, forward_less), (AD_LESS, adjoint_less)):
        power, block = (damping, each(jnp.ones_like, damping))
        total = each(jnp.zeros_like, damping)
        for b in range(8):
            taken = ((count >> b) & 1) == 1
            total = each(lambda s, v, q: jnp.where(taken, v + q * s, s), total, block, power)
            if b < 7:
                block = each(lambda v, q: v + v * q, block, power)
                power = each(lambda q: q * q, power)
        store(total, field, slot)

    head = load(field, HEAD)
    push = each(
        lambda f, d, g, h: f - d * (g - h), load(field, STATE), load(field, DAMPING), load(grid, FORWARD), head
    )
    store(push, field, SOURCE)
    store(
        each(
            lambda w, u, h, e: w * u + (h + (1.0 - not_first) * e),
            load(field, FW_LESS),
            push,
            head,
            load(grid, ADJOINT),
        ),
        field,
        STATE,
    )
    v, alpha = (load(field, STATE), None)
    for n in range(COARSEN - 1):
        at = COARSEN - 2 - n
        misfit = each(lambda f: f / COARSEN, load(points, at))
        alpha = adjoint_step(misfit if alpha is None else each(jnp.add, alpha, misfit))
        v = forward_step(each(jnp.add, v, load(grid, CONTROL)))
        store(v, coarse_points, n)
    store(alpha, field, ALPHA)

    damping = load(field, DAMPING)
    alpha, beta, gamma = (load(field, ALPHA), load(field, BETA), load(field, GAMMA))
    keep = each(
        lambda g, d, a, h: g + not_last * (d * a) + h, gamma, damping, alpha, load(field, HEAD_ADJOINT)
    )
    pull = each(lambda k, d, g, b: d * (k - g) + b, keep, damping, load(grid, ADJOINT), beta)
    push = load(field, SOURCE)
    less = load(field, AD_LESS)
    store(
        each(lambda a, k, w, q, d: not_last * a + k + not_first * ((1.0 + d * w) * q), alpha, keep, less, pull, damping),
        field,
        TOTAL,
    )
    rest = each(lambda a, k, w, q: not_last * a + not_first * (k + w * q), alpha, keep, less, pull)
    store(
        each(
            lambda t, w, d, u, h, o: t + (not_last * ((1.0 + d * w) * u) + h - o) / COARSEN,
            rest,
            load(field, FW_LESS),
            damping,
            push,
            load(field, HEAD),
            load(grid, TARGET),
        ),
        field,
        GAMMA,
    )
    store(pull, field, BETA)
    store(keep, field, STATE)

    v, total = (load(field, GAMMA), load(field, TOTAL))
    for n in range(COARSEN - 1):
        v = adjoint_step(v)
        total = each(jnp.add, total, v)
        if n < COARSEN - 2:
            at = COARSEN - 2 - n
            v = each(lambda a, f, o: a + (f - o) / COARSEN, v, load(coarse_points, at), load(grid, TARGET))
    store(total, field, TOTAL)

    for n, slot in enumerate((SOURCE, BETA, ALPHA, TOTAL)):
        for p in range(PHASES):
            for t in range(TILES):
                raw[n, t, pl.ds(p, 4, stride=PHASES), :] = field[slot, p, t, 0:4, :]
    for n in range(4):
        for t in range(TILES):
            for h in range(2):
                chan_ref[2 * t + h, n] = raw[n, t, 8 * h : 8 * h + 8, :]
    for n, slot in enumerate((HEAD, STATE)):
        for p in range(PHASES):
            for t in range(TILES):
                at = (n * TILES + t) * ROWS + p
                keep_ref[pl.ds(at, 4, stride=PHASES), :] = field[slot, p, t, 0:4, :]


def owned_damping(own_ref):
    owner = lax.axis_index("tm_2")
    rows = own_ref[REACTION, pl.ds(pl.multiple_of(8 * (owner % 2), 8), 8), :]
    reaction = rows[:, 0:LANES]
    for t in range(1, TILES):
        reaction = jnp.where(owner // 2 == t, rows[:, t * LANES : (t + 1) * LANES], reaction)
    return 1.0 / (1.0 + COARSEN * reaction)


def block_kernel(got_ref, own_ref, totals_ref, local_ref):
    d = owned_damping(own_ref)
    block = lax.axis_index("tm_0") * 8 + lax.axis_index("tm_1")
    even = lax.axis_index("tm_3") == 0

    def source(n, i):
        return got_ref[i % 2, i // 2, n]

    zero = jnp.zeros_like(d)
    forward, adjoint, shifted = ([zero], [zero], [zero])
    for i in range(BLOCK):
        forward.append(d * forward[i] + source(0, i))
        shifted.append(source(2, i))
    for i in range(BLOCK - 1, -1, -1):
        adjoint.append(d * adjoint[-1] + source(1, i))
    adjoint = adjoint[::-1][1:]
    gradient = [source(3, i) for i in range(BLOCK)]
    while len(gradient) > 1:
        gradient = [a + b for a, b in zip(gradient[::2], gradient[1::2])]
    whole = d * adjoint[0] + source(1, 0)
    for b in range(BLOCKS):
        totals_ref[b, 0] = jnp.where(b > block, forward[BLOCK], whole)
        totals_ref[b, 1] = shifted[BLOCK]
        totals_ref[b, 2] = gradient[0]
    for y in range(BLOCK // 2):
        for n, values in enumerate((forward, adjoint, shifted)):
            local_ref[y, n] = jnp.where(even, values[2 * y], values[2 * y + 1])


def spread_kernel(totals_ref, local_ref, own_ref, out_ref):
    d = owned_damping(own_ref)
    block = lax.axis_index("tm_0") * 8 + lax.axis_index("tm_1")
    even = lax.axis_index("tm_3") == 0
    d2 = d * d
    d4 = d2 * d2
    d16 = (d4 * d4) * (d4 * d4)
    entry = jnp.zeros_like(d)
    for b in range(BLOCKS - 1):
        entry = jnp.where(b < block, d16 * entry + totals_ref[b, 0], entry)
    after = jnp.zeros_like(d)
    for b in range(BLOCKS - 1, 0, -1):
        after = jnp.where(b > block, d16 * after + totals_ref[b, 0], after)
    before = jnp.where(block > 0, totals_ref[jnp.maximum(block - 1, 0), 1], 0.0)
    gradient = [totals_ref[b, 2] for b in range(BLOCKS)]
    while len(gradient) > 1:
        gradient = [a + b for a, b in zip(gradient[::2], gradient[1::2])]
    gradient = gradient[0] * (1.0 / (COARSEN * SLABS))
    entry = jnp.where(even, entry, d * entry)
    after = jnp.where(even, d * after, after)
    half = BLOCK // 2
    for y in range(half):
        out_ref[y, 0] = local_ref[y, 0] + entry
        out_ref[y, 2] = gradient
        entry = d2 * entry
    for y in range(half - 1, -1, -1):
        shifted = local_ref[y, 2]
        if y == 0:
            shifted = jnp.where(even, before, shifted)
        out_ref[y, 1] = (local_ref[y, 1] + after) + shifted
        after = d2 * after


def finish_kernel(got_ref, keep_ref, order_ref, forward_ref, adjoint_ref, gradient_ref):
    def rows(n, h):
        return jnp.concatenate([got_ref[2 * t + h, n] for t in range(TILES)], 1)

    head, keep = (
        jnp.concatenate([keep_ref[pl.ds((n * TILES + t) * ROWS, ROWS), :] for t in range(TILES)], 1) for n in range(2)
    )
    forward, adjoint, gradient = (jnp.concatenate([rows(n, 0), rows(n, 1)], 0) for n in range(3))
    parts = jnp.concatenate([forward + head, adjoint + keep, gradient], 0)
    parts = reorder(parts, order_ref[...])
    forward_ref[...] = parts[0:ROWS]
    adjoint_ref[...] = parts[ROWS : 2 * ROWS]
    gradient_ref[...] = parts[2 * ROWS : 3 * ROWS]


def in_vmem(count):
    return [pl.BlockSpec(memory_space=pltpu.VMEM)] * count


def tiles(*lead):
    return pltpu.VMEM((*lead, 8, LANES), jnp.float32)


def in_place(value):
    return pltpu.with_memory_space_constraint(value, pltpu.VMEM)


def field_shape(*lead):
    return pltpu.VMEM((*lead, PHASES, TILES, 8, LANES), jnp.float32)


def relax_scratch():
    return [
        pltpu.VMEM((ARRAYS, TILES, 2 * ROWS, LANES), jnp.float32),
        field_shape(ARRAYS),
        field_shape(11),
        pltpu.VMEM((2, PHASES, TILES + 2 * SWEEPS, 8, LANES), jnp.float32),
        field_shape(COARSEN),
        field_shape(COARSEN),
    ]


def shards(control, initial, diffusion, reaction, forward_guess, adjoint_guess, observed):
    own, order = pl.pallas_call(
        pack_kernel,
        out_shape=(pltpu.VMEM((ARRAYS, ROWS, COLS), jnp.float32), pltpu.VMEM((COLS, COLS), jnp.bfloat16)),
        in_specs=[pl.BlockSpec(memory_space=pl.ANY)] * 7,
        out_specs=in_vmem(2),
        scratch_shapes=[
            pltpu.VMEM((ARRAYS, ROWS, COLS), jnp.float32),
            pltpu.VMEM((COLS, COLS), jnp.bfloat16),
            pltpu.SemaphoreType.DMA((ARRAYS,)),
        ],
        name="pack",
    )(control, initial, diffusion, reaction, forward_guess[0], adjoint_guess[0], observed[0])
    both = in_place(lax.all_gather(own, "space", axis=0))
    own = in_place(own)
    block = jax.ShapeDtypeStruct((ROWS, COLS), jnp.float32)
    channels, keep = pl.pallas_call(
        relax_kernel,
        out_shape=(tiles(8, 4), pltpu.VMEM((128, LANES), jnp.float32)),
        in_specs=in_vmem(2),
        out_specs=in_vmem(2),
        scratch_shapes=relax_scratch(),
        name="relax",
    )(own, both)
    got = lax.all_to_all(channels, "tm_2", 0, 0, tiled=True)
    got = in_place(lax.all_gather(got, "tm_3", axis=0))
    totals, local = pl.pallas_call(
        block_kernel,
        out_shape=(tiles(BLOCKS, 3), tiles(8, 3)),
        in_specs=in_vmem(2),
        out_specs=in_vmem(2),
        name="block",
    )(got, own)
    totals = in_place(lax.all_to_all(totals, ("tm_0", "tm_1"), 0, 0, tiled=True))
    sent = pl.pallas_call(
        spread_kernel, out_shape=tiles(8, 3), in_specs=in_vmem(3), out_specs=in_vmem(1)[0], name="spread"
    )(totals, in_place(local), own)
    back = in_place(lax.all_to_all(sent, "tm_2", 0, 0, tiled=True))
    keep, order = in_place(keep), in_place(order)
    forward_states, adjoint_states, gradient = pl.pallas_call(
        finish_kernel, out_shape=(block, block, block), in_specs=in_vmem(3), out_specs=in_vmem(3), name="finish"
    )(back, keep, order)
    return (forward_states[None], adjoint_states[None], gradient)


def solution(mesh):
    finer = Mesh(
        mesh.devices.reshape(2, 8, 8, 2, mesh.shape["space"]),
        ("tm_0", "tm_1", "tm_2", "tm_3", "space"),
    )
    return jax.shard_map(
        shards,
        mesh=finer,
        in_specs=(
            P("space", None),
            P("space", None),
            P("space", None),
            P("space", None),
            P(TM, "space", None),
            P(TM, "space", None),
            P(TM, "space", None),
        ),
        out_specs=(P(TM, "space", None), P(TM, "space", None), P("space", None)),
        check_vma=False,
    )
```

```python
import jax
import jax.numpy as jnp
from jax import lax
from jax.experimental import pallas as pl
from jax.experimental.pallas import tpu as pltpu
from jax.sharding import Mesh
from jax.sharding import PartitionSpec as P

SWEEPS = 3
COARSEN = 8
SLABS = 256
TM = ("tm_0", "tm_1", "tm_2", "tm_3")
ROWS = 16
COLS = 512
LANES = 128
TILES = COLS // LANES
PHASES = 4
BLOCK = 16
BLOCKS = SLABS // BLOCK

FORWARD, ADJOINT, TARGET, CONTROL, SPREAD, REACTION = range(6)
ARRAYS = 6
DAMPING, ALPHA, BETA, GAMMA, SOURCE, STATE, TOTAL, FW_LESS, AD_LESS, HEAD, HEAD_ADJOINT = range(11)


def tm_index():
    return ((lax.axis_index("tm_0") * 8 + lax.axis_index("tm_1")) * 8 + lax.axis_index("tm_2")) * 2 + lax.axis_index(
        "tm_3"
    )


def space_index():
    return lax.axis_index("space")


def each(fn, *fields):
    return [[fn(*cells) for cells in zip(*rows)] for rows in zip(*fields)]


def load(ref, *at):
    return [[ref[(*at, p, t)] for t in range(TILES)] for p in range(PHASES)]


def store(value, ref, *at):
    for p, row in enumerate(value):
        for t, cell in enumerate(row):
            ref[(*at, p, t)] = cell


def trim(field, count):
    return [row[count : len(row) - count] for row in field]


def inside():
    lane = lax.broadcasted_iota(jnp.int32, (8, LANES), 1)
    left, right = (jnp.where(lane == edge, 0.0, 1.0) for edge in (0, LANES - 1))
    return [[left] * SWEEPS + [jnp.ones_like(left)] * TILES + [right] * SWEEPS] * PHASES


def make_stencil(space):
    sub = lax.broadcasted_iota(jnp.int32, (8, LANES), 0)
    lane = lax.broadcasted_iota(jnp.int32, (8, LANES), 1)
    up_ok = sub != 4 * space
    down_ok = sub != 7 - 4 * space
    first, last = (lane == 0, lane == LANES - 1)

    def widen(field):
        out = []
        for row in field:
            left = [pltpu.roll(cell, 1, 1) for cell in row[TILES - SWEEPS :]]
            right = [pltpu.roll(cell, LANES - 1, 1) for cell in row[:SWEEPS]]
            left[-1] = jnp.where(first, 0.0, left[-1])
            right[0] = jnp.where(last, 0.0, right[0])
            out.append(left + row + right)
        return out

    def neighbours(field):
        above = [jnp.where(up_ok, pltpu.roll(cell, 1, 0), 0.0) for cell in field[-1][1:-1]]
        below = [jnp.where(down_ok, pltpu.roll(cell, 7, 0), 0.0) for cell in field[0][1:-1]]
        out = []
        pairs = [[u + a for u, a in zip(above, field[0][:-2])]]
        for p in range(1, PHASES):
            pairs.append([u + a for u, a in zip(field[p - 1][1:], field[p][:-1])])
        pairs.append([b + d for b, d in zip(field[-1][2:], below)])
        for p in range(PHASES):
            upper = pairs[p][:-1] if p else pairs[p]
            lower = pairs[p + 1][1:] if p < PHASES - 1 else pairs[p + 1]
            out.append([x + y for x, y in zip(upper, lower)])
        return out

    return widen, neighbours


def exact_terms(value):
    high = value.astype(jnp.bfloat16)
    rest = value - high.astype(jnp.float32)
    middle = rest.astype(jnp.bfloat16)
    low = (rest - middle.astype(jnp.float32)).astype(jnp.bfloat16)
    return high, middle, low


def reorder(value, selection):
    high, middle, low = (
        jnp.dot(term, selection, preferred_element_type=jnp.float32)
        for term in exact_terms(value)
    )
    return high + (middle + low)


def pack_kernel(control, initial, diffusion, reaction, forward, adjoint, observed, out_ref, order_ref, raw, into, sems):
    is_first = tm_index() == 0

    def copy(source, slot):
        return pltpu.make_async_copy(source, raw.at[slot], sems.at[slot])

    @pl.when(is_first)
    def _():
        copy(initial, ADJOINT).start()

    @pl.when(jnp.logical_not(is_first))
    def _():
        copy(adjoint, ADJOINT).start()

    rest = (
        (forward, FORWARD),
        (observed, TARGET),
        (control, CONTROL),
        (diffusion, SPREAD),
        (reaction, REACTION),
    )
    for source, slot in rest:
        copy(source, slot).start()
    column, lane = (lax.broadcasted_iota(jnp.int32, (LANES, COLS), d) for d in (1, 0))
    for t in range(TILES):
        order_ref[t * LANES : (t + 1) * LANES, :] = jnp.where(column == TILES * lane + t, 1.0, 0.0).astype(jnp.bfloat16)
    column, lane = (lax.broadcasted_iota(jnp.int32, (COLS, LANES), d) for d in (0, 1))
    for t in range(TILES):
        into[:, t * LANES : (t + 1) * LANES] = jnp.where(column == TILES * lane + t, 1.0, 0.0).astype(jnp.bfloat16)
    copy(adjoint, ADJOINT).wait()
    for source, slot in rest:
        copy(source, slot).wait()
    packed = reorder(raw[...].reshape(ARRAYS * ROWS, COLS), into[...])
    out_ref[...] = packed.reshape(ARRAYS, ROWS, COLS)


def relax_kernel(own_ref, both_ref, chan_ref, keep_ref, raw, grid, field, wide, points, coarse_points):
    slab = tm_index()
    space = space_index()
    widen, neighbours = make_stencil(space)
    not_last = jnp.where(slab == SLABS - 1, 0.0, 1.0)
    not_first = jnp.where(slab == 0, 0.0, 1.0)

    for n in range(ARRAYS):
        for t in range(TILES):
            cols = pl.ds(t * LANES, LANES)
            raw[n, t, 0:ROWS, :] = own_ref[n, :, cols]
            raw[n, t, ROWS : 2 * ROWS, :] = both_ref[1 - space, n, :, cols]
    for n in range(ARRAYS):
        for p in range(PHASES):
            for t in range(TILES):
                grid[n, p, t] = raw[n, t, pl.ds(p, 8, stride=PHASES), :]

    spread, reaction = (load(grid, SPREAD), load(grid, REACTION))
    inverse = each(lambda s, r: 1.0 / (1.0 + 4.0 * s + r), spread, reaction)
    store(each(jnp.multiply, inside(), widen(inverse)), wide, 0)
    store(each(jnp.multiply, inside(), widen(each(jnp.multiply, spread, inverse))), wide, 1)
    damping = each(lambda r: 1.0 / (1.0 + COARSEN * r), reaction)
    store(damping, field, DAMPING)

    def inverse_wide(count):
        return [[wide[0, p, t] for t in range(SWEEPS - count, SWEEPS + TILES + count)] for p in range(PHASES)]

    def weight_wide(count):
        return [[wide[1, p, t] for t in range(SWEEPS - count, SWEEPS + TILES + count)] for p in range(PHASES)]

    def forward_step(right_side):
        v = widen(right_side)
        scaled = each(jnp.multiply, inverse_wide(SWEEPS - 1), trim(v, 1))
        for n in range(SWEEPS):
            v = each(
                lambda s, w, q: s + w * q, trim(scaled, n), weight_wide(SWEEPS - 1 - n), neighbours(v)
            )
        return v

    def adjoint_step(y):
        carried, summed = (widen(each(jnp.multiply, weight_wide(0), y)), y)
        for n in range(SWEEPS - 1):
            carried = neighbours(carried)
            summed = each(jnp.add, summed, trim(carried, SWEEPS - 1 - n))
            carried = each(jnp.multiply, weight_wide(SWEEPS - 1 - n), carried)
        final = neighbours(carried)
        return each(lambda s, i, f: s * i + f, summed, inverse_wide(0), final)

    zeros = each(jnp.zeros_like, damping)
    store(zeros, field, HEAD)
    store(zeros, field, HEAD_ADJOINT)

    @pl.when(slab == 0)
    def _():
        store(load(grid, ADJOINT), field, HEAD)

        def head_body(i, _):
            v = forward_step(each(jnp.add, load(field, HEAD), load(grid, CONTROL)))
            store(v, field, HEAD)
            store(v, coarse_points, i)
            return 0

        def head_adjoint_body(n, _):
            at = COARSEN - 2 - n
            v = each(lambda a, f: a + f / COARSEN, load(field, HEAD_ADJOINT), load(coarse_points, at))
            store(adjoint_step(v), field, HEAD_ADJOINT)
            return 0

        lax.fori_loop(0, COARSEN, head_body, 0)
        lax.fori_loop(0, COARSEN - 1, head_adjoint_body, 0)

    v, beta = (load(grid, FORWARD), load(grid, ADJOINT))
    gamma = each(lambda g: g / COARSEN, load(grid, FORWARD))
    for i in range(COARSEN):
        v = forward_step(each(jnp.add, v, load(grid, CONTROL)))
        store(v, points, i)
        beta = adjoint_step(beta)
        gamma = adjoint_step(each(lambda a, o: a - o / COARSEN, gamma, load(grid, TARGET)))
    store(v, field, STATE)
    store(beta, field, BETA)
    store(gamma, field, GAMMA)

    forward_less = jnp.maximum(SLABS - 2 - slab, 0)
    adjoint_less = jnp.maximum(slab - 1, 0)
    counts = (forward_less, adjoint_less)
    power, block = (damping, each(jnp.ones_like, damping))
    sums = [each(jnp.zeros_like, damping) for _ in counts]
    for b in range(8):
        for n, count in enumerate(counts):
            taken = ((count >> b) & 1) == 1
            sums[n] = each(lambda s, v, q: jnp.where(taken, v + q * s, s), sums[n], block, power)
        if b < 7:
            block = each(lambda v, q: v + v * q, block, power)
            power = each(lambda q: q * q, power)
    store(sums[0], field, FW_LESS)
    store(sums[1], field, AD_LESS)

    head = load(field, HEAD)
    push = each(
        lambda f, d, g, h: f - d * (g - h), load(field, STATE), load(field, DAMPING), load(grid, FORWARD), head
    )
    store(push, field, SOURCE)
    store(
        each(
            lambda w, u, h, e: w * u + (h + (1.0 - not_first) * e),
            load(field, FW_LESS),
            push,
            head,
            load(grid, ADJOINT),
        ),
        field,
        STATE,
    )
    v, alpha = (load(field, STATE), None)
    for n in range(COARSEN - 1):
        at = COARSEN - 2 - n
        misfit = each(lambda f: f / COARSEN, load(points, at))
        alpha = adjoint_step(misfit if alpha is None else each(jnp.add, alpha, misfit))
        v = forward_step(each(jnp.add, v, load(grid, CONTROL)))
        store(v, coarse_points, n)
    store(alpha, field, ALPHA)

    damping = load(field, DAMPING)
    alpha, beta, gamma = (load(field, ALPHA), load(field, BETA), load(field, GAMMA))
    keep = each(
        lambda g, d, a, h: g + not_last * (d * a) + h, gamma, damping, alpha, load(field, HEAD_ADJOINT)
    )
    pull = each(lambda k, d, g, b: d * (k - g) + b, keep, damping, load(grid, ADJOINT), beta)
    push = load(field, SOURCE)
    less = load(field, AD_LESS)
    store(
        each(lambda a, k, w, q, d: not_last * a + k + not_first * ((1.0 + d * w) * q), alpha, keep, less, pull, damping),
        field,
        TOTAL,
    )
    rest = each(lambda a, k, w, q: not_last * a + not_first * (k + w * q), alpha, keep, less, pull)
    store(
        each(
            lambda t, w, d, u, h, o: t + (not_last * ((1.0 + d * w) * u) + h - o) / COARSEN,
            rest,
            load(field, FW_LESS),
            damping,
            push,
            load(field, HEAD),
            load(grid, TARGET),
        ),
        field,
        GAMMA,
    )
    store(pull, field, BETA)
    store(keep, field, STATE)

    v, total = (load(field, GAMMA), load(field, TOTAL))
    for n in range(COARSEN - 1):
        v = adjoint_step(v)
        total = each(jnp.add, total, v)
        if n < COARSEN - 2:
            at = COARSEN - 2 - n
            v = each(lambda a, f, o: a + (f - o) / COARSEN, v, load(coarse_points, at), load(grid, TARGET))
    store(total, field, TOTAL)

    for n, slot in enumerate((SOURCE, BETA, ALPHA, TOTAL)):
        for p in range(PHASES):
            for t in range(TILES):
                raw[n, t, pl.ds(p, 4, stride=PHASES), :] = field[slot, p, t, 0:4, :]
    for n in range(4):
        for t in range(TILES):
            for h in range(2):
                chan_ref[2 * t + h, n] = raw[n, t, 8 * h : 8 * h + 8, :]
    for n, slot in enumerate((HEAD, STATE)):
        for p in range(PHASES):
            for t in range(TILES):
                at = (n * TILES + t) * ROWS + p
                keep_ref[pl.ds(at, 4, stride=PHASES), :] = field[slot, p, t, 0:4, :]


def owned_damping(own_ref):
    owner = lax.axis_index("tm_2")
    rows = own_ref[REACTION, pl.ds(pl.multiple_of(8 * (owner % 2), 8), 8), :]
    reaction = rows[:, 0:LANES]
    for t in range(1, TILES):
        reaction = jnp.where(owner // 2 == t, rows[:, t * LANES : (t + 1) * LANES], reaction)
    return 1.0 / (1.0 + COARSEN * reaction)


def block_kernel(got_ref, own_ref, totals_ref, local_ref):
    d = owned_damping(own_ref)
    block = lax.axis_index("tm_0") * 8 + lax.axis_index("tm_1")
    even = lax.axis_index("tm_3") == 0

    def source(n, i):
        return got_ref[i % 2, i // 2, n]

    zero = jnp.zeros_like(d)
    forward, adjoint, shifted = ([zero], [zero], [zero])
    for i in range(BLOCK):
        forward.append(d * forward[i] + source(0, i))
        shifted.append(source(2, i))
    for i in range(BLOCK - 1, -1, -1):
        adjoint.append(d * adjoint[-1] + source(1, i))
    adjoint = adjoint[::-1][1:]
    gradient = [source(3, i) for i in range(BLOCK)]
    while len(gradient) > 1:
        gradient = [a + b for a, b in zip(gradient[::2], gradient[1::2])]
    whole = d * adjoint[0] + source(1, 0)
    for b in range(BLOCKS):
        totals_ref[b, 0] = jnp.where(b > block, forward[BLOCK], whole)
        totals_ref[b, 1] = shifted[BLOCK]
        totals_ref[b, 2] = gradient[0]
    for y in range(BLOCK // 2):
        for n, values in enumerate((forward, adjoint, shifted)):
            local_ref[y, n] = jnp.where(even, values[2 * y], values[2 * y + 1])


def spread_kernel(totals_ref, local_ref, own_ref, out_ref):
    d = owned_damping(own_ref)
    block = lax.axis_index("tm_0") * 8 + lax.axis_index("tm_1")
    even = lax.axis_index("tm_3") == 0
    d2 = d * d
    d4 = d2 * d2
    d16 = (d4 * d4) * (d4 * d4)
    entry = jnp.zeros_like(d)
    for b in range(BLOCKS - 1):
        entry = jnp.where(b < block, d16 * entry + totals_ref[b, 0], entry)
    after = jnp.zeros_like(d)
    for b in range(BLOCKS - 1, 0, -1):
        after = jnp.where(b > block, d16 * after + totals_ref[b, 0], after)
    before = jnp.where(block > 0, totals_ref[jnp.maximum(block - 1, 0), 1], 0.0)
    gradient = [totals_ref[b, 2] for b in range(BLOCKS)]
    while len(gradient) > 1:
        gradient = [a + b for a, b in zip(gradient[::2], gradient[1::2])]
    gradient = gradient[0] * (1.0 / (COARSEN * SLABS))
    entry = jnp.where(even, entry, d * entry)
    after = jnp.where(even, d * after, after)
    half = BLOCK // 2
    for y in range(half):
        out_ref[y, 0] = local_ref[y, 0] + entry
        out_ref[y, 2] = gradient
        entry = d2 * entry
    for y in range(half - 1, -1, -1):
        shifted = local_ref[y, 2]
        if y == 0:
            shifted = jnp.where(even, before, shifted)
        out_ref[y, 1] = (local_ref[y, 1] + after) + shifted
        after = d2 * after


def finish_kernel(got_ref, keep_ref, order_ref, forward_ref, adjoint_ref, gradient_ref):
    def rows(n, h):
        return jnp.concatenate([got_ref[2 * t + h, n] for t in range(TILES)], 1)

    head, keep = (
        jnp.concatenate([keep_ref[pl.ds((n * TILES + t) * ROWS, ROWS), :] for t in range(TILES)], 1) for n in range(2)
    )
    forward, adjoint, gradient = (jnp.concatenate([rows(n, 0), rows(n, 1)], 0) for n in range(3))
    parts = jnp.concatenate([forward + head, adjoint + keep, gradient], 0)
    parts = reorder(parts, order_ref[...])
    forward_ref[...] = parts[0:ROWS]
    adjoint_ref[...] = parts[ROWS : 2 * ROWS]
    gradient_ref[...] = parts[2 * ROWS : 3 * ROWS]


def in_vmem(count):
    return [pl.BlockSpec(memory_space=pltpu.VMEM)] * count


def tiles(*lead):
    return pltpu.VMEM((*lead, 8, LANES), jnp.float32)


def in_place(value):
    return pltpu.with_memory_space_constraint(value, pltpu.VMEM)


def field_shape(*lead):
    return pltpu.VMEM((*lead, PHASES, TILES, 8, LANES), jnp.float32)


def relax_scratch():
    return [
        pltpu.VMEM((ARRAYS, TILES, 2 * ROWS, LANES), jnp.float32),
        field_shape(ARRAYS),
        field_shape(11),
        pltpu.VMEM((2, PHASES, TILES + 2 * SWEEPS, 8, LANES), jnp.float32),
        field_shape(COARSEN),
        field_shape(COARSEN),
    ]


def shards(control, initial, diffusion, reaction, forward_guess, adjoint_guess, observed):
    own, order = pl.pallas_call(
        pack_kernel,
        out_shape=(pltpu.VMEM((ARRAYS, ROWS, COLS), jnp.float32), pltpu.VMEM((COLS, COLS), jnp.bfloat16)),
        in_specs=[pl.BlockSpec(memory_space=pl.ANY)] * 7,
        out_specs=in_vmem(2),
        scratch_shapes=[
            pltpu.VMEM((ARRAYS, ROWS, COLS), jnp.float32),
            pltpu.VMEM((COLS, COLS), jnp.bfloat16),
            pltpu.SemaphoreType.DMA((ARRAYS,)),
        ],
        name="pack",
    )(control, initial, diffusion, reaction, forward_guess[0], adjoint_guess[0], observed[0])
    both = in_place(lax.all_gather(own, "space", axis=0))
    own = in_place(own)
    block = jax.ShapeDtypeStruct((ROWS, COLS), jnp.float32)
    channels, keep = pl.pallas_call(
        relax_kernel,
        out_shape=(tiles(8, 4), pltpu.VMEM((128, LANES), jnp.float32)),
        in_specs=in_vmem(2),
        out_specs=in_vmem(2),
        scratch_shapes=relax_scratch(),
        name="relax",
    )(own, both)
    got = lax.all_to_all(channels, "tm_2", 0, 0, tiled=True)
    got = in_place(lax.all_gather(got, "tm_3", axis=0))
    totals, local = pl.pallas_call(
        block_kernel,
        out_shape=(tiles(BLOCKS, 3), tiles(8, 3)),
        in_specs=in_vmem(2),
        out_specs=in_vmem(2),
        name="block",
    )(got, own)
    totals = in_place(lax.all_to_all(totals, ("tm_0", "tm_1"), 0, 0, tiled=True))
    sent = pl.pallas_call(
        spread_kernel, out_shape=tiles(8, 3), in_specs=in_vmem(3), out_specs=in_vmem(1)[0], name="spread"
    )(totals, in_place(local), own)
    back = in_place(lax.all_to_all(sent, "tm_2", 0, 0, tiled=True))
    keep, order = in_place(keep), in_place(order)
    forward_states, adjoint_states, gradient = pl.pallas_call(
        finish_kernel, out_shape=(block, block, block), in_specs=in_vmem(3), out_specs=in_vmem(3), name="finish"
    )(back, keep, order)
    return (forward_states[None], adjoint_states[None], gradient)


def solution(mesh):
    finer = Mesh(
        mesh.devices.reshape(2, 8, 8, 2, mesh.shape["space"]),
        ("tm_0", "tm_1", "tm_2", "tm_3", "space"),
    )
    return jax.shard_map(
        shards,
        mesh=finer,
        in_specs=(
            P("space", None),
            P("space", None),
            P("space", None),
            P("space", None),
            P(TM, "space", None),
            P(TM, "space", None),
            P(TM, "space", None),
        ),
        out_specs=(P(TM, "space", None), P(TM, "space", None), P("space", None)),
        check_vma=False,
    )
```

```python
import jax
import jax.numpy as jnp
from jax import lax
from jax.experimental import pallas as pl
from jax.experimental.pallas import tpu as pltpu
from jax.sharding import Mesh
from jax.sharding import PartitionSpec as P

SWEEPS = 3
COARSEN = 8
SLABS = 256
TM = ("tm_0", "tm_1", "tm_2", "tm_3")
ROWS = 16
COLS = 512
LANES = 128
TILES = COLS // LANES
PHASES = 4
BLOCK = 16
BLOCKS = SLABS // BLOCK

FORWARD, ADJOINT, TARGET, CONTROL, SPREAD, REACTION = range(6)
ARRAYS = 6
DAMPING, ALPHA, BETA, GAMMA, SOURCE, STATE, TOTAL, FW_LESS, AD_LESS, HEAD, HEAD_ADJOINT = range(11)


def tm_index():
    return ((lax.axis_index("tm_0") * 8 + lax.axis_index("tm_1")) * 8 + lax.axis_index("tm_2")) * 2 + lax.axis_index(
        "tm_3"
    )


def space_index():
    return lax.axis_index("space")


def each(fn, *fields):
    return [[fn(*cells) for cells in zip(*rows)] for rows in zip(*fields)]


def load(ref, *at):
    return [[ref[(*at, p, t)] for t in range(TILES)] for p in range(PHASES)]


def store(value, ref, *at):
    for p, row in enumerate(value):
        for t, cell in enumerate(row):
            ref[(*at, p, t)] = cell


def trim(field, count):
    return [row[count : len(row) - count] for row in field]


def inside():
    lane = lax.broadcasted_iota(jnp.int32, (8, LANES), 1)
    left, right = (jnp.where(lane == edge, 0.0, 1.0) for edge in (0, LANES - 1))
    return [[left] * SWEEPS + [jnp.ones_like(left)] * TILES + [right] * SWEEPS] * PHASES


def make_stencil(space):
    sub = lax.broadcasted_iota(jnp.int32, (8, LANES), 0)
    lane = lax.broadcasted_iota(jnp.int32, (8, LANES), 1)
    up_ok = sub != 4 * space
    down_ok = sub != 7 - 4 * space
    first, last = (lane == 0, lane == LANES - 1)

    def widen(field):
        out = []
        for row in field:
            left = [pltpu.roll(cell, 1, 1) for cell in row[TILES - SWEEPS :]]
            right = [pltpu.roll(cell, LANES - 1, 1) for cell in row[:SWEEPS]]
            left[-1] = jnp.where(first, 0.0, left[-1])
            right[0] = jnp.where(last, 0.0, right[0])
            out.append(left + row + right)
        return out

    def neighbours(field):
        above = [jnp.where(up_ok, pltpu.roll(cell, 1, 0), 0.0) for cell in field[-1][1:-1]]
        below = [jnp.where(down_ok, pltpu.roll(cell, 7, 0), 0.0) for cell in field[0][1:-1]]
        out = []
        pairs = [[u + a for u, a in zip(above, field[0][:-2])]]
        for p in range(1, PHASES):
            pairs.append([u + a for u, a in zip(field[p - 1][1:], field[p][:-1])])
        pairs.append([b + d for b, d in zip(field[-1][2:], below)])
        for p in range(PHASES):
            upper = pairs[p][:-1] if p else pairs[p]
            lower = pairs[p + 1][1:] if p < PHASES - 1 else pairs[p + 1]
            out.append([x + y for x, y in zip(upper, lower)])
        return out

    return widen, neighbours


def exact_terms(value):
    high = value.astype(jnp.bfloat16)
    rest = value - high.astype(jnp.float32)
    middle = rest.astype(jnp.bfloat16)
    low = (rest - middle.astype(jnp.float32)).astype(jnp.bfloat16)
    return high, middle, low


def reorder(value, selection):
    count = value.shape[0]
    terms = jnp.dot(jnp.concatenate(exact_terms(value), 0), selection, preferred_element_type=jnp.float32)
    high, middle, low = (terms[n * count : (n + 1) * count] for n in range(3))
    return high + (middle + low)


def pack_kernel(control, initial, diffusion, reaction, forward, adjoint, observed, out_ref, order_ref, raw, into, sems):
    is_first = tm_index() == 0

    def copy(source, slot):
        return pltpu.make_async_copy(source, raw.at[slot], sems.at[slot])

    @pl.when(is_first)
    def _():
        copy(initial, ADJOINT).start()

    @pl.when(jnp.logical_not(is_first))
    def _():
        copy(adjoint, ADJOINT).start()

    rest = (
        (forward, FORWARD),
        (observed, TARGET),
        (control, CONTROL),
        (diffusion, SPREAD),
        (reaction, REACTION),
    )
    for source, slot in rest:
        copy(source, slot).start()
    column, lane = (lax.broadcasted_iota(jnp.int32, (LANES, COLS), d) for d in (1, 0))
    for t in range(TILES):
        order_ref[t * LANES : (t + 1) * LANES, :] = jnp.where(column == TILES * lane + t, 1.0, 0.0).astype(jnp.bfloat16)
    column, lane = (lax.broadcasted_iota(jnp.int32, (COLS, LANES), d) for d in (0, 1))
    for t in range(TILES):
        into[:, t * LANES : (t + 1) * LANES] = jnp.where(column == TILES * lane + t, 1.0, 0.0).astype(jnp.bfloat16)
    copy(adjoint, ADJOINT).wait()
    for source, slot in rest:
        copy(source, slot).wait()
    packed = reorder(raw[...].reshape(ARRAYS * ROWS, COLS), into[...])
    out_ref[...] = packed.reshape(ARRAYS, ROWS, COLS)


def relax_kernel(own_ref, both_ref, chan_ref, keep_ref, raw, grid, field, wide, points, coarse_points):
    slab = tm_index()
    space = space_index()
    widen, neighbours = make_stencil(space)
    not_last = jnp.where(slab == SLABS - 1, 0.0, 1.0)
    not_first = jnp.where(slab == 0, 0.0, 1.0)

    for n in range(ARRAYS):
        for t in range(TILES):
            cols = pl.ds(t * LANES, LANES)
            raw[n, t, 0:ROWS, :] = own_ref[n, :, cols]
            raw[n, t, ROWS : 2 * ROWS, :] = both_ref[1 - space, n, :, cols]
    for n in range(ARRAYS):
        for p in range(PHASES):
            for t in range(TILES):
                grid[n, p, t] = raw[n, t, pl.ds(p, 8, stride=PHASES), :]

    spread, reaction = (load(grid, SPREAD), load(grid, REACTION))
    inverse = each(lambda s, r: 1.0 / (1.0 + 4.0 * s + r), spread, reaction)
    store(each(jnp.multiply, inside(), widen(inverse)), wide, 0)
    store(each(jnp.multiply, inside(), widen(each(jnp.multiply, spread, inverse))), wide, 1)
    damping = each(lambda r: 1.0 / (1.0 + COARSEN * r), reaction)
    store(damping, field, DAMPING)

    def inverse_wide(count):
        return [[wide[0, p, t] for t in range(SWEEPS - count, SWEEPS + TILES + count)] for p in range(PHASES)]

    def weight_wide(count):
        return [[wide[1, p, t] for t in range(SWEEPS - count, SWEEPS + TILES + count)] for p in range(PHASES)]

    def forward_step(right_side):
        v = widen(right_side)
        scaled = each(jnp.multiply, inverse_wide(SWEEPS - 1), trim(v, 1))
        for n in range(SWEEPS):
            v = each(
                lambda s, w, q: s + w * q, trim(scaled, n), weight_wide(SWEEPS - 1 - n), neighbours(v)
            )
        return v

    def adjoint_step(y):
        carried, summed = (widen(each(jnp.multiply, weight_wide(0), y)), y)
        for n in range(SWEEPS - 1):
            carried = neighbours(carried)
            summed = each(jnp.add, summed, trim(carried, SWEEPS - 1 - n))
            carried = each(jnp.multiply, weight_wide(SWEEPS - 1 - n), carried)
        final = neighbours(carried)
        return each(lambda s, i, f: s * i + f, summed, inverse_wide(0), final)

    v, beta = (load(grid, FORWARD), load(grid, ADJOINT))
    gamma = each(lambda g: g / COARSEN, load(grid, FORWARD))
    for i in range(COARSEN):
        v = forward_step(each(jnp.add, v, load(grid, CONTROL)))
        store(v, points, i)
        beta = adjoint_step(beta)
        gamma = adjoint_step(each(lambda a, o: a - o / COARSEN, gamma, load(grid, TARGET)))
    store(v, field, STATE)
    store(beta, field, BETA)
    store(gamma, field, GAMMA)

    zeros = each(jnp.zeros_like, damping)
    store(zeros, field, HEAD)
    store(zeros, field, HEAD_ADJOINT)

    @pl.when(slab == 0)
    def _():
        store(load(grid, ADJOINT), field, HEAD)

        def head_body(i, _):
            v = forward_step(each(jnp.add, load(field, HEAD), load(grid, CONTROL)))
            store(v, field, HEAD)
            store(v, coarse_points, i)
            return 0

        def head_adjoint_body(n, _):
            at = COARSEN - 2 - n
            v = each(lambda a, f: a + f / COARSEN, load(field, HEAD_ADJOINT), load(coarse_points, at))
            store(adjoint_step(v), field, HEAD_ADJOINT)
            return 0

        lax.fori_loop(0, COARSEN, head_body, 0)
        lax.fori_loop(0, COARSEN - 1, head_adjoint_body, 0)

    forward_less = jnp.maximum(SLABS - 2 - slab, 0)
    adjoint_less = jnp.maximum(slab - 1, 0)
    for slot, count in ((FW_LESS, forward_less), (AD_LESS, adjoint_less)):
        power, block = (damping, each(jnp.ones_like, damping))
        total = each(jnp.zeros_like, damping)
        for b in range(8):
            taken = ((count >> b) & 1) == 1
            total = each(lambda s, v, q: jnp.where(taken, v + q * s, s), total, block, power)
            if b < 7:
                block = each(lambda v, q: v + v * q, block, power)
                power = each(lambda q: q * q, power)
        store(total, field, slot)

    head = load(field, HEAD)
    push = each(
        lambda f, d, g, h: f - d * (g - h), load(field, STATE), load(field, DAMPING), load(grid, FORWARD), head
    )
    store(push, field, SOURCE)
    store(
        each(
            lambda w, u, h, e: w * u + (h + (1.0 - not_first) * e),
            load(field, FW_LESS),
            push,
            head,
            load(grid, ADJOINT),
        ),
        field,
        STATE,
    )
    v, alpha = (load(field, STATE), None)
    for n in range(COARSEN - 1):
        at = COARSEN - 2 - n
        misfit = each(lambda f: f / COARSEN, load(points, at))
        alpha = adjoint_step(misfit if alpha is None else each(jnp.add, alpha, misfit))
        v = forward_step(each(jnp.add, v, load(grid, CONTROL)))
        store(v, coarse_points, n)
    store(alpha, field, ALPHA)

    damping = load(field, DAMPING)
    alpha, beta, gamma = (load(field, ALPHA), load(field, BETA), load(field, GAMMA))
    keep = each(
        lambda g, d, a, h: g + not_last * (d * a) + h, gamma, damping, alpha, load(field, HEAD_ADJOINT)
    )
    pull = each(lambda k, d, g, b: d * (k - g) + b, keep, damping, load(grid, ADJOINT), beta)
    push = load(field, SOURCE)
    less = load(field, AD_LESS)
    store(
        each(lambda a, k, w, q, d: not_last * a + k + not_first * ((1.0 + d * w) * q), alpha, keep, less, pull, damping),
        field,
        TOTAL,
    )
    rest = each(lambda a, k, w, q: not_last * a + not_first * (k + w * q), alpha, keep, less, pull)
    store(
        each(
            lambda t, w, d, u, h, o: t + (not_last * ((1.0 + d * w) * u) + h - o) / COARSEN,
            rest,
            load(field, FW_LESS),
            damping,
            push,
            load(field, HEAD),
            load(grid, TARGET),
        ),
        field,
        GAMMA,
    )
    store(pull, field, BETA)
    store(keep, field, STATE)

    v, total = (load(field, GAMMA), load(field, TOTAL))
    for n in range(COARSEN - 1):
        v = adjoint_step(v)
        total = each(jnp.add, total, v)
        if n < COARSEN - 2:
            at = COARSEN - 2 - n
            v = each(lambda a, f, o: a + (f - o) / COARSEN, v, load(coarse_points, at), load(grid, TARGET))
    store(total, field, TOTAL)

    for n, slot in enumerate((SOURCE, BETA, ALPHA, TOTAL)):
        for p in range(PHASES):
            for t in range(TILES):
                raw[n, t, pl.ds(p, 4, stride=PHASES), :] = field[slot, p, t, 0:4, :]
    for n in range(4):
        for t in range(TILES):
            for h in range(2):
                chan_ref[2 * t + h, n] = raw[n, t, 8 * h : 8 * h + 8, :]
    for n, slot in enumerate((HEAD, STATE)):
        for p in range(PHASES):
            for t in range(TILES):
                at = (n * TILES + t) * ROWS + p
                keep_ref[pl.ds(at, 4, stride=PHASES), :] = field[slot, p, t, 0:4, :]


def owned_damping(own_ref):
    owner = lax.axis_index("tm_2")
    rows = own_ref[REACTION, pl.ds(pl.multiple_of(8 * (owner % 2), 8), 8), :]
    reaction = rows[:, 0:LANES]
    for t in range(1, TILES):
        reaction = jnp.where(owner // 2 == t, rows[:, t * LANES : (t + 1) * LANES], reaction)
    return 1.0 / (1.0 + COARSEN * reaction)


def block_kernel(got_ref, own_ref, totals_ref, local_ref):
    d = owned_damping(own_ref)
    block = lax.axis_index("tm_0") * 8 + lax.axis_index("tm_1")
    even = lax.axis_index("tm_3") == 0

    def source(n, i):
        return got_ref[i % 2, i // 2, n]

    zero = jnp.zeros_like(d)
    forward, adjoint, shifted = ([zero], [zero], [zero])
    for i in range(BLOCK):
        forward.append(d * forward[i] + source(0, i))
        shifted.append(source(2, i))
    for i in range(BLOCK - 1, -1, -1):
        adjoint.append(d * adjoint[-1] + source(1, i))
    adjoint = adjoint[::-1][1:]
    gradient = [source(3, i) for i in range(BLOCK)]
    while len(gradient) > 1:
        gradient = [a + b for a, b in zip(gradient[::2], gradient[1::2])]
    whole = d * adjoint[0] + source(1, 0)
    for b in range(BLOCKS):
        totals_ref[b, 0] = jnp.where(b > block, forward[BLOCK], whole)
        totals_ref[b, 1] = shifted[BLOCK]
        totals_ref[b, 2] = gradient[0]
    for y in range(BLOCK // 2):
        for n, values in enumerate((forward, adjoint, shifted)):
            local_ref[y, n] = jnp.where(even, values[2 * y], values[2 * y + 1])


def spread_kernel(totals_ref, local_ref, own_ref, out_ref):
    d = owned_damping(own_ref)
    block = lax.axis_index("tm_0") * 8 + lax.axis_index("tm_1")
    even = lax.axis_index("tm_3") == 0
    d2 = d * d
    d4 = d2 * d2
    d16 = (d4 * d4) * (d4 * d4)
    entry = jnp.zeros_like(d)
    for b in range(BLOCKS - 1):
        entry = jnp.where(b < block, d16 * entry + totals_ref[b, 0], entry)
    after = jnp.zeros_like(d)
    for b in range(BLOCKS - 1, 0, -1):
        after = jnp.where(b > block, d16 * after + totals_ref[b, 0], after)
    before = jnp.where(block > 0, totals_ref[jnp.maximum(block - 1, 0), 1], 0.0)
    gradient = [totals_ref[b, 2] for b in range(BLOCKS)]
    while len(gradient) > 1:
        gradient = [a + b for a, b in zip(gradient[::2], gradient[1::2])]
    gradient = gradient[0] * (1.0 / (COARSEN * SLABS))
    entry = jnp.where(even, entry, d * entry)
    after = jnp.where(even, d * after, after)
    half = BLOCK // 2
    for y in range(half):
        out_ref[y, 0] = local_ref[y, 0] + entry
        out_ref[y, 2] = gradient
        entry = d2 * entry
    for y in range(half - 1, -1, -1):
        shifted = local_ref[y, 2]
        if y == 0:
            shifted = jnp.where(even, before, shifted)
        out_ref[y, 1] = (local_ref[y, 1] + after) + shifted
        after = d2 * after


def finish_kernel(got_ref, keep_ref, order_ref, forward_ref, adjoint_ref, gradient_ref):
    def rows(n, h):
        return jnp.concatenate([got_ref[2 * t + h, n] for t in range(TILES)], 1)

    head, keep = (
        jnp.concatenate([keep_ref[pl.ds((n * TILES + t) * ROWS, ROWS), :] for t in range(TILES)], 1) for n in range(2)
    )
    forward, adjoint, gradient = (jnp.concatenate([rows(n, 0), rows(n, 1)], 0) for n in range(3))
    parts = jnp.concatenate([forward + head, adjoint + keep, gradient], 0)
    parts = reorder(parts, order_ref[...])
    forward_ref[...] = parts[0:ROWS]
    adjoint_ref[...] = parts[ROWS : 2 * ROWS]
    gradient_ref[...] = parts[2 * ROWS : 3 * ROWS]


def in_vmem(count):
    return [pl.BlockSpec(memory_space=pltpu.VMEM)] * count


def tiles(*lead):
    return pltpu.VMEM((*lead, 8, LANES), jnp.float32)


def in_place(value):
    return pltpu.with_memory_space_constraint(value, pltpu.VMEM)


def field_shape(*lead):
    return pltpu.VMEM((*lead, PHASES, TILES, 8, LANES), jnp.float32)


def relax_scratch():
    return [
        pltpu.VMEM((ARRAYS, TILES, 2 * ROWS, LANES), jnp.float32),
        field_shape(ARRAYS),
        field_shape(11),
        pltpu.VMEM((2, PHASES, TILES + 2 * SWEEPS, 8, LANES), jnp.float32),
        field_shape(COARSEN),
        field_shape(COARSEN),
    ]


def shards(control, initial, diffusion, reaction, forward_guess, adjoint_guess, observed):
    own, order = pl.pallas_call(
        pack_kernel,
        out_shape=(pltpu.VMEM((ARRAYS, ROWS, COLS), jnp.float32), pltpu.VMEM((COLS, COLS), jnp.bfloat16)),
        in_specs=[pl.BlockSpec(memory_space=pl.ANY)] * 7,
        out_specs=in_vmem(2),
        scratch_shapes=[
            pltpu.VMEM((ARRAYS, ROWS, COLS), jnp.float32),
            pltpu.VMEM((COLS, COLS), jnp.bfloat16),
            pltpu.SemaphoreType.DMA((ARRAYS,)),
        ],
        name="pack",
    )(control, initial, diffusion, reaction, forward_guess[0], adjoint_guess[0], observed[0])
    both = in_place(lax.all_gather(own, "space", axis=0))
    own = in_place(own)
    block = jax.ShapeDtypeStruct((ROWS, COLS), jnp.float32)
    channels, keep = pl.pallas_call(
        relax_kernel,
        out_shape=(tiles(8, 4), pltpu.VMEM((128, LANES), jnp.float32)),
        in_specs=in_vmem(2),
        out_specs=in_vmem(2),
        scratch_shapes=relax_scratch(),
        name="relax",
    )(own, both)
    got = lax.all_to_all(channels, "tm_2", 0, 0, tiled=True)
    got = in_place(lax.all_gather(got, "tm_3", axis=0))
    totals, local = pl.pallas_call(
        block_kernel,
        out_shape=(tiles(BLOCKS, 3), tiles(8, 3)),
        in_specs=in_vmem(2),
        out_specs=in_vmem(2),
        name="block",
    )(got, own)
    totals = in_place(lax.all_to_all(totals, ("tm_0", "tm_1"), 0, 0, tiled=True))
    sent = pl.pallas_call(
        spread_kernel, out_shape=tiles(8, 3), in_specs=in_vmem(3), out_specs=in_vmem(1)[0], name="spread"
    )(totals, in_place(local), own)
    back = in_place(lax.all_to_all(sent, "tm_2", 0, 0, tiled=True))
    keep, order = in_place(keep), in_place(order)
    forward_states, adjoint_states, gradient = pl.pallas_call(
        finish_kernel, out_shape=(block, block, block), in_specs=in_vmem(3), out_specs=in_vmem(3), name="finish"
    )(back, keep, order)
    return (forward_states[None], adjoint_states[None], gradient)


def solution(mesh):
    finer = Mesh(
        mesh.devices.reshape(2, 8, 8, 2, mesh.shape["space"]),
        ("tm_0", "tm_1", "tm_2", "tm_3", "space"),
    )
    return jax.shard_map(
        shards,
        mesh=finer,
        in_specs=(
            P("space", None),
            P("space", None),
            P("space", None),
            P("space", None),
            P(TM, "space", None),
            P(TM, "space", None),
            P(TM, "space", None),
        ),
        out_specs=(P(TM, "space", None), P(TM, "space", None), P("space", None)),
        check_vma=False,
    )
```
